32 devices in a mesh: rep: 8 (over z, x), grp: 4 (over y, core).
Axes of the slice: x: 2, y: 2, z: 4, core: 2. Of those that a mesh axis runs over, the one named last changes fastest.
Arguments:
- tokens: bfloat16 [8, 512, 1088], P('rep', 'grp'), may hold values from -24 to 24
- segments: int32 [8, 512], P('rep'), may hold values from 0 to 3, never falling along the last dimension, each value on 1 to 256 neighbouring positions
- cotangent: bfloat16 [8, 512, 1088], P('rep', 'grp'), may hold values from -6 to 6
- packed_weight: bfloat16 [1088, 3264], P('grp')
- output_weight: bfloat16 [1088, 1088], P('grp'), may hold values from -0.5 to 0.5
- up_weight: bfloat16 [1088, 4352], P('grp'), may hold values from -0.1875 to 0.1875
- down_weight: bfloat16 [4352, 1088], P('grp'), may hold values from -0.09375 to 0.09375
- first_gain: bfloat16 [1088], P('grp'), may hold values from 0.099609375 to 1.8984375
- first_shift: bfloat16 [1088], P('grp'), may hold values from -3 to 3
- query_bias: bfloat16 [1088], P('grp'), may hold values from -3 to 3
- value_bias: bfloat16 [1088], P('grp'), may hold values from -3 to 3
- output_bias: bfloat16 [1088], P('grp'), may hold values from -3 to 3
- second_gain: bfloat16 [1088], P('grp'), may hold values from 0.099609375 to 1.8984375
- second_shift: bfloat16 [1088], P('grp'), may hold values from -3 to 3
- hidden_bias: bfloat16 [4352], P('grp'), may hold values from -3 to 3
- down_bias: bfloat16 [1088], P('grp'), may hold values from -3 to 3
Outputs:
- layer_out: float32 [8, 512, 1088], P('rep', 'grp')
- grad_tokens: float32 [8, 512, 1088], P('rep', 'grp')
- grad_packed_weight: float32 [1088, 3264], P('grp', 'rep')
- grad_output_weight: float32 [1088, 1088], P('grp', 'rep')
- grad_up_weight: float32 [1088, 4352], P('grp', 'rep')
- grad_down_weight: float32 [4352, 1088], P('grp', 'rep')
- grad_first_gain: float32 [1088], replicated
- grad_first_shift: float32 [1088], replicated
- grad_query_bias: float32 [1088], replicated
- grad_value_bias: float32 [1088], replicated
- grad_output_bias: float32 [1088], replicated
- grad_second_gain: float32 [1088], replicated
- grad_second_shift: float32 [1088], replicated
- grad_hidden_bias: float32 [4352], replicated
- grad_down_bias: float32 [1088], replicated
The draws below stay inside these ranges and needn't reach their ends.
Inputs may be any that keep to these rules, and one draw needn't show every extreme that they name: `segments`: within each sequence the document numbers never fall, every number appears, and each document has at most 256 tokens; some document has exactly that many.
All inputs are finite; a program needn't handle non-finite values.
Results may differ from the reference program's by a relative error of at most 0.02.
The reference program's roundings to bfloat16 on the way count: a program that leaves them out, or rounds other values in their place, can miss the bound.
Values may be sent and summed in bfloat16 or wider, within the bound.
No kernel may reach another device: no remote copies, remote signals or barrier semaphores. Data moves between devices by JAX's collectives and lax.ppermute only.
A program may use at most 256 MiB of HBM per device.

```python
import math
import jax
import jax.numpy as jnp
import numpy as np
from jax import lax

D = 1088
HEADS = 17
HD = 64
FF = 4352
SEG_COUNT = 4
SEQ = 512
SEQS = 8
SEG_MOST = 256


def draw_tokens(key, part):
    base_key, row_key, col_key = jax.random.split(jax.random.fold_in(key, 11), 3)
    base_draw = jnp.clip(jax.random.normal(base_key, (SEQS, SEQ, D), jnp.float32), -4.0, 4.0)
    row_scale = jnp.exp(jax.random.uniform(row_key, (SEQS, SEQ, 1), jnp.float32, math.log(0.3), math.log(3.0)))
    col_scale = jnp.exp(jax.random.uniform(col_key, (1, 1, D), jnp.float32, math.log(0.5), math.log(2.0)))
    return (base_draw * row_scale * col_scale).astype(jnp.bfloat16)


def draw_packed_weight(key, part):
    query_key, key_key, value_key = jax.random.split(jax.random.fold_in(key, 23), 3)
    fan_scale = 1.0 / math.sqrt(D)
    query_draw = jnp.clip(jax.random.normal(query_key, (D, D), jnp.float32), -4.0, 4.0) * fan_scale
    key_draw = jnp.clip(jax.random.normal(key_key, (D, D), jnp.float32), -4.0, 4.0) * fan_scale
    value_draw = jnp.clip(jax.random.normal(value_key, (D, D), jnp.float32), -4.0, 4.0) * fan_scale
    return jnp.concatenate([query_draw, key_draw, value_draw], axis=1).astype(jnp.bfloat16)


def strengthened(array, rng, source, target, shards_of, factor):
    def block_of(axis_at):
        return (jnp.arange(array.shape[axis_at]) // (array.shape[axis_at] // shards_of)).reshape((-1,) + (1,) * (array.ndim - 1 - axis_at))

    first = jax.random.permutation(rng, shards_of)[block_of(target)]
    far = (block_of(target) + shards_of // 2) % shards_of
    return jnp.where((block_of(source) == first) | (block_of(source) == far), factor * array, array)


def steps_of(key, dims, cuts, least, largest):
    factor_of = 1.0
    for dim, blocks in cuts:
        steps = jax.random.uniform(jax.random.fold_in(jax.random.fold_in(key, 6), dim), (blocks,), jnp.float32, least / len(cuts), largest / len(cuts))
        factor_of = factor_of * jnp.repeat(jnp.exp(steps), dims[dim] // blocks).reshape((-1,) + (1,) * (len(dims) - 1 - dim))
    return factor_of


def length_profile(amount, total, reach, skew):
    portions = [(1 << 20) // math.isqrt(rank ** skew) + 1 for rank in range(2, amount + 1)]
    spare, given = total - reach - (amount - 1), [1] * (amount - 1)
    while spare > 0:
        free = [i for i in range(amount - 1) if given[i] < reach]
        mass, budget = sum([portions[i] for i in free]), spare
        for i in free:
            extra = min(reach - given[i], max(1, budget * portions[i] // mass), spare)
            given[i] = given[i] + extra
            spare = spare - extra
    return np.array([reach] + given)


def ragged(key, count, total, reach, lean):
    if count == 2:
        one = jax.random.randint(key, (), max(1, total - reach), min(reach, total - 1) + 1)
        return jnp.stack([one, total - one])
    tallies = jnp.asarray(length_profile(count, total, reach, lean), jnp.int32)
    couples = (count - 1) // 2
    source_of, sink = tallies[1:1 + 2 * couples:2], tallies[2:2 + 2 * couples:2]
    room = jnp.minimum(source_of - 1, reach - sink)
    passed = jax.random.randint(jax.random.fold_in(key, 1), (couples,), 0, 1 << 20) % (room + 1)
    tallies = tallies.at[1:1 + 2 * couples:2].set(source_of - passed).at[2:2 + 2 * couples:2].set(sink + passed)
    return tallies[jax.random.permutation(jax.random.fold_in(key, 2), count)]


def normal_values(rng, extent, spread, most, pieces=(), kind=jnp.bfloat16):
    gain = steps_of(rng, extent, pieces, -0.22, 0.18) if pieces else 1.0
    result = jax.random.normal(rng, extent, jnp.float32) * spread * gain
    return jnp.minimum(jnp.maximum(result, -most), most).astype(kind)


def noise_with(own_key, shape, scale, reach, cuts, heavy, kind=jnp.bfloat16):
    array = scale * jax.random.normal(own_key, shape, jnp.float32)
    if cuts:
        array = array * steps_of(own_key, shape, cuts, -0.22, 0.18)
    return jnp.clip(strengthened(array, jax.random.fold_in(own_key, 3), *heavy), -reach, reach).astype(kind)


def setup_inputs(seed: int = 0) -> dict:
    arg_keys = jax.random.split(jax.random.key(seed), 17)
    return {
        "tokens": draw_tokens(jax.random.fold_in(arg_keys[16], 71), 0),
        "segments": jax.vmap(lambda own: jnp.searchsorted(jnp.cumsum(ragged(own, SEG_COUNT, SEQ, SEG_MOST, 2)), jnp.arange(SEQ), side="right"))(jax.random.split(arg_keys[1], SEQS)).reshape((SEQS, SEQ)).astype(jnp.int32),
        "cotangent": noise_with(arg_keys[2], (SEQS, SEQ, D), 1.0, 6.0, ((0, 8), (1, 4)), (0, 2, 8, 2.0)),
        "packed_weight": draw_packed_weight(jax.random.fold_in(arg_keys[16], 71), 0),
        "output_weight": normal_values(arg_keys[4], (D, D), (D // 8) ** -0.5, 0.5, ((0, 4),)),
        "up_weight": normal_values(arg_keys[5], (D, FF), D ** -0.5, 0.1875, ((0, 4),)),
        "down_weight": normal_values(arg_keys[6], (FF, D), FF ** -0.5, 0.09375, ((0, 4),)),
        "first_gain": jnp.clip(1.0 + 0.18 * jax.random.normal(arg_keys[7], (D,), jnp.float32), 0.099609375, 1.8984375).astype(jnp.bfloat16),
        "first_shift": normal_values(arg_keys[8], (D,), 0.5, 3.0, ((0, 4),)),
        "query_bias": normal_values(arg_keys[9], (D,), 0.5, 3.0, ((0, 4),)),
        "value_bias": normal_values(arg_keys[10], (D,), 0.5, 3.0, ((0, 4),)),
        "output_bias": normal_values(arg_keys[11], (D,), 0.5, 3.0, ((0, 4),)),
        "second_gain": jnp.clip(1.0 + 0.18 * jax.random.normal(arg_keys[12], (D,), jnp.float32), 0.099609375, 1.8984375).astype(jnp.bfloat16),
        "second_shift": normal_values(arg_keys[13], (D,), 0.5, 3.0, ((0, 4),)),
        "hidden_bias": normal_values(arg_keys[14], (FF,), 0.5, 3.0, ((0, 4),)),
        "down_bias": normal_values(arg_keys[15], (D,), 0.5, 3.0, ((0, 4),)),
    }


epsilon = 1e-05
gelu_factor = 0.7978845608028654
masked_score = -1e+30

def gelu_parts(pre_act):
    inner = gelu_factor * (pre_act + 0.044715 * pre_act * pre_act * pre_act)
    tanh_value = jnp.tanh(inner)
    gelu_value = 0.5 * pre_act * (1.0 + tanh_value)
    gelu_slope = 0.5 * (1.0 + tanh_value) + 0.5 * pre_act * (1.0 - tanh_value * tanh_value) * gelu_factor * (1.0 + 3.0 * 0.044715 * pre_act * pre_act)
    return (gelu_value, gelu_slope)

def norm_rows(field):
    row_mean = lax.optimization_barrier(jnp.mean(field, axis=-1, keepdims=True))
    centered = field - row_mean
    inv_std = lax.rsqrt(lax.optimization_barrier(jnp.mean(centered * centered, axis=-1, keepdims=True)) + epsilon)
    return (centered * inv_std, inv_std)

def norm_back(grad_out, normed, inv_std, gain_row):
    scaled = grad_out * gain_row
    return inv_std * (scaled - lax.optimization_barrier(jnp.mean(scaled, axis=-1, keepdims=True)) - normed * lax.optimization_barrier(jnp.mean(scaled * normed, axis=-1, keepdims=True)))

def split_heads(rows):
    return rows.astype(jnp.float32).reshape(rows.shape[0], HEADS, HD)

def head_scores(query_rows, key_rows, allowed):
    scores = jnp.einsum('qhd,khd->hqk', split_heads(query_rows), split_heads(key_rows)) * (1.0 / math.sqrt(HD))
    return jnp.where(allowed[None, :, :], scores, masked_score)

def attend_forward(query_rows, key_rows, value_rows, allowed):
    scores = head_scores(query_rows, key_rows, allowed)
    row_max = lax.optimization_barrier(jnp.max(scores, axis=2, keepdims=True))
    log_total = row_max + jnp.log(lax.optimization_barrier(jnp.sum(jnp.exp(scores - row_max), axis=2, keepdims=True)))
    attn_probs = jnp.exp(scores - log_total).astype(jnp.bfloat16)
    mixed = jnp.einsum('hqk,khd->qhd', attn_probs.astype(jnp.float32), split_heads(value_rows))
    return (mixed.reshape(query_rows.shape[0], D).astype(jnp.bfloat16), log_total)

def attend_backward(query_rows, key_rows, value_rows, allowed, log_total, mixed_heads, grad_mixed):
    scores = head_scores(query_rows, key_rows, allowed)
    probs_float = jnp.exp(scores - log_total)
    probs_low = probs_float.astype(jnp.bfloat16).astype(jnp.float32)
    grad_heads = split_heads(grad_mixed)
    row_delta = jnp.einsum('qhd,qhd->hq', grad_heads, split_heads(mixed_heads))
    grad_values = jnp.einsum('hqk,qhd->khd', probs_low, grad_heads)
    grad_probs = jnp.einsum('qhd,khd->hqk', grad_heads, split_heads(value_rows))
    grad_scores = (probs_float * (grad_probs - row_delta[:, :, None]) * (1.0 / math.sqrt(HD))).astype(jnp.bfloat16).astype(jnp.float32)
    grad_query = jnp.einsum('hqk,khd->qhd', grad_scores, split_heads(key_rows))
    grad_keys = jnp.einsum('hqk,qhd->khd', grad_scores, split_heads(query_rows))
    return (grad_query.reshape(query_rows.shape[0], D), grad_keys.reshape(key_rows.shape[0], D), grad_values.reshape(key_rows.shape[0], D))

def one_sequence(parameters, rows_in, segment_ids, grad_rows):
    packed_weight, output_weight, up_weight, down_weight, first_gain, first_shift, query_bias, value_bias, output_bias, second_gain, second_shift, hidden_bias, down_bias = parameters
    rows_float = rows_in.astype(jnp.float32)
    normed_first, inv_first = norm_rows(rows_float)
    gain_first = first_gain.astype(jnp.float32)
    normal_a = (normed_first * gain_first + first_shift.astype(jnp.float32)).astype(jnp.bfloat16)
    projected = jnp.dot(normal_a, packed_weight, preferred_element_type=jnp.float32)
    query_rows = (projected[:, :D] + query_bias.astype(jnp.float32)).astype(jnp.bfloat16)
    key_rows = projected[:, D:2 * D].astype(jnp.bfloat16)
    value_rows = (projected[:, 2 * D:] + value_bias.astype(jnp.float32)).astype(jnp.bfloat16)
    positions = jnp.arange(SEQ, dtype=jnp.int32)
    allowed = (positions[None, :] <= positions[:, None]) & (segment_ids[None, :] == segment_ids[:, None])
    mixed_heads, log_total = attend_forward(query_rows, key_rows, value_rows, allowed)
    residual = rows_float + jnp.dot(mixed_heads, output_weight, preferred_element_type=jnp.float32) + output_bias.astype(jnp.float32)
    normed_second, inv_second = norm_rows(residual)
    gain_second = second_gain.astype(jnp.float32)
    normal_c = (normed_second * gain_second + second_shift.astype(jnp.float32)).astype(jnp.bfloat16)
    pre_act = jnp.dot(normal_c, up_weight, preferred_element_type=jnp.float32) + hidden_bias.astype(jnp.float32)
    gelu_value, gelu_slope = gelu_parts(pre_act)
    hidden = gelu_value.astype(jnp.bfloat16)
    layer_rows = residual + jnp.dot(hidden, down_weight, preferred_element_type=jnp.float32) + down_bias.astype(jnp.float32)
    grad_float = grad_rows.astype(jnp.float32)
    grad_down = jnp.dot(hidden.T, grad_rows, preferred_element_type=jnp.float32)
    grad_down_bias = lax.optimization_barrier(jnp.sum(grad_float, axis=0))
    grad_hidden = jnp.dot(grad_rows, down_weight.T, preferred_element_type=jnp.float32)
    grad_pre = (grad_hidden * gelu_slope).astype(jnp.bfloat16)
    grad_up = jnp.dot(normal_c.T, grad_pre, preferred_element_type=jnp.float32)
    grad_hidden_bias = lax.optimization_barrier(jnp.sum(grad_pre.astype(jnp.float32), axis=0))
    grad_c = jnp.dot(grad_pre, up_weight.T, preferred_element_type=jnp.float32)
    grad_second_gain = lax.optimization_barrier(jnp.sum(grad_c * normed_second, axis=0))
    grad_second_shift = lax.optimization_barrier(jnp.sum(grad_c, axis=0))
    grad_resid = grad_float + norm_back(grad_c, normed_second, inv_second, gain_second)
    grad_attn = grad_resid.astype(jnp.bfloat16)
    grad_output = jnp.dot(mixed_heads.T, grad_attn, preferred_element_type=jnp.float32)
    grad_output_bias = lax.optimization_barrier(jnp.sum(grad_attn.astype(jnp.float32), axis=0))
    grad_mixed = jnp.dot(grad_attn, output_weight.T, preferred_element_type=jnp.float32).astype(jnp.bfloat16)
    grad_query, grad_keys, grad_values = attend_backward(query_rows, key_rows, value_rows, allowed, log_total, mixed_heads, grad_mixed)
    grad_packed_rows = jnp.concatenate([grad_query.astype(jnp.bfloat16), grad_keys.astype(jnp.bfloat16), grad_values.astype(jnp.bfloat16)], axis=1)
    grad_packed = jnp.dot(normal_a.T, grad_packed_rows, preferred_element_type=jnp.float32)
    grad_query_bias = lax.optimization_barrier(jnp.sum(grad_packed_rows[:, :D].astype(jnp.float32), axis=0))
    grad_value_bias = lax.optimization_barrier(jnp.sum(grad_packed_rows[:, 2 * D:].astype(jnp.float32), axis=0))
    grad_a = jnp.dot(grad_packed_rows, packed_weight.T, preferred_element_type=jnp.float32)
    grad_first_gain = lax.optimization_barrier(jnp.sum(grad_a * normed_first, axis=0))
    grad_first_shift = lax.optimization_barrier(jnp.sum(grad_a, axis=0))
    grad_in = grad_resid + norm_back(grad_a, normed_first, inv_first, gain_first)
    grads = (grad_packed, grad_output, grad_up, grad_down, grad_first_gain, grad_first_shift, grad_query_bias, grad_value_bias, grad_output_bias, grad_second_gain, grad_second_shift, grad_hidden_bias, grad_down_bias)
    return (layer_rows, grad_in, grads)

def reference(tokens, segments, cotangent, packed_weight, output_weight, up_weight, down_weight, first_gain, first_shift, query_bias, value_bias, output_bias, second_gain, second_shift, hidden_bias, down_bias):
    parameters = (packed_weight, output_weight, up_weight, down_weight, first_gain, first_shift, query_bias, value_bias, output_bias, second_gain, second_shift, hidden_bias, down_bias)
    zero_grads = tuple((jnp.zeros(weight_arg.shape, jnp.float32) for weight_arg in parameters))

    def scan_step(totals, inputs):
        rows_in, segment_ids, grad_rows = inputs
        layer_rows, grad_in, grads = one_sequence(parameters, rows_in, segment_ids, grad_rows)
        return (jax.tree.map(jnp.add, totals, grads), (layer_rows, grad_in))
    totals, (layer_out, grad_tokens) = lax.scan(scan_step, zero_grads, (tokens, segments, cotangent))
    return (layer_out, grad_tokens, totals[0], totals[1], totals[2], totals[3], totals[4], totals[5], totals[6], totals[7], totals[8], totals[9], totals[10], totals[11], totals[12])
```

```python
import functools
import math

import jax
import jax.numpy as jnp
from jax import lax
from jax.experimental import pallas as pl
from jax.experimental.pallas import tpu as pltpu
from jax.sharding import PartitionSpec as P

D = 1088
HEADS = 17
HD = 64

epsilon = 1e-05
gelu_factor = 0.7978845608028654
masked_score = -1e30
f32 = jnp.float32
bf16 = jnp.bfloat16


def gelu_parts(pre_act):
    inner = gelu_factor * (pre_act + 0.044715 * pre_act * pre_act * pre_act)
    tanh_value = jnp.tanh(inner)
    gelu_value = 0.5 * pre_act * (1.0 + tanh_value)
    gelu_slope = 0.5 * (1.0 + tanh_value) + 0.5 * pre_act * (
        1.0 - tanh_value * tanh_value
    ) * gelu_factor * (1.0 + 3.0 * 0.044715 * pre_act * pre_act)
    return (gelu_value, gelu_slope)


def norm_rows(field):
    row_mean = jnp.mean(field, axis=-1, keepdims=True)
    centered = field - row_mean
    inv_std = lax.rsqrt(jnp.mean(centered * centered, axis=-1, keepdims=True) + epsilon)
    return (centered * inv_std, inv_std)


def norm_back(grad_out, normed, inv_std, gain_row):
    scaled = grad_out * gain_row
    return inv_std * (
        scaled
        - jnp.mean(scaled, axis=-1, keepdims=True)
        - normed * jnp.mean(scaled * normed, axis=-1, keepdims=True)
    )


def contract(left, right, left_dim, right_dim):
    return lax.dot_general(
        left, right, (((left_dim,), (right_dim,)), ((), ())), preferred_element_type=f32
    )


def swap(value, axis, size, bit):
    return lax.ppermute(value, axis, [(i, i ^ bit) for i in range(size)])


def log2(count):
    return count.bit_length() - 1


def group_gather(own, size):
    blocks = [own]
    for j in range(1, size):
        low = j & -j
        blocks.append(swap(blocks[j ^ low], "grp", size, low))
    return blocks


def group_scatter_sum(blocks, size):
    blocks = list(blocks)
    bit = 1
    while bit < size:
        for j in reversed(range(0, size, 2 * bit)):
            moved = swap(blocks[j + bit].astype(bf16), "grp", size, bit)
            blocks[j] = blocks[j] + moved.astype(f32)
        bit *= 2
    return blocks[0]


def place_rows(blocks, rank):
    rows = blocks[0].shape[0]
    whole = jnp.zeros((rows * len(blocks),) + blocks[0].shape[1:], blocks[0].dtype)
    for j, block in enumerate(blocks):
        whole = lax.dynamic_update_slice_in_dim(whole, block, (rank ^ j) * rows, 0)
    return whole


def token_blocks(rows, size):
    count = rows.shape[0] // size
    return [rows[j * count : (j + 1) * count] for j in range(size)]


def sum_everywhere(vector, reps, size):
    for axis, count in (("grp", size), ("rep", reps)):
        bit = 1
        while bit < count:
            vector = vector + swap(vector, axis, count, bit)
            bit *= 2
    return vector


def halve_rows(value, bit, reps, axis):
    mine = (lax.axis_index("rep") >> bit) & 1
    half = value.shape[axis] // 2
    keep = lax.dynamic_slice_in_dim(value, mine * half, half, axis)
    give = lax.dynamic_slice_in_dim(value, (1 - mine) * half, half, axis).astype(bf16)
    return keep + swap(give, "rep", reps, 1 << bit).astype(f32)


def halve_lanes(value, bit, reps):
    mine = ((lax.axis_index("rep") >> bit) & 1) == 1
    half = value.shape[-1] // 2
    low, high = value[..., :half], value[..., half:]
    give = jnp.where(mine, low, high).astype(bf16)
    return jnp.where(mine, high, low) + swap(give, "rep", reps, 1 << bit).astype(f32)


def scatter_natural(value, reps):
    bits = log2(reps)
    rest = value.shape[0] // reps
    value = value.reshape((2,) * bits + (rest,) + value.shape[1:])
    for bit in range(bits):
        value = halve_rows(value, bit, reps, bits - 1 - bit)
        value = lax.squeeze(value, (bits - 1 - bit,))
    return value


def scatter_pieces(value, reps, size, row_axis):
    row_bits = log2(reps // size)
    for bit in range(log2(reps)):
        if bit < row_bits:
            value = halve_rows(value, bit, reps, row_axis)
        else:
            value = halve_lanes(value, bit, reps)
    return value


def piece_of(rep, reps, size):
    row_bits, all_bits = log2(reps // size), log2(reps)
    row_part, lane_part = 0, 0
    for bit in range(all_bits):
        taken = (rep >> bit) & 1
        if bit < row_bits:
            row_part = 2 * row_part + taken
        else:
            lane_part = 2 * lane_part + taken
    return row_part, lane_part


def match_rounds(reps, kinds):
    left = {v: set(range(kinds)) for v in range(reps)}
    rounds = []
    for _ in range(kinds):
        owner = {}

        def place(v, seen):
            for kind in sorted(left[v]):
                target = (reps * kind + v) // kinds
                if target in seen:
                    continue
                seen.add(target)
                if target not in owner or place(owner[target][0], seen):
                    owner[target] = (v, kind)
                    return True
            return False

        for v in range(reps):
            place(v, set())
        chosen = [0] * reps
        for v, kind in owner.values():
            chosen[v] = kind
            left[v].discard(kind)
        rounds.append(chosen)
    return rounds


def mask_bias(bias_ref, bounds_ref, base_ref):
    tokens = bias_ref.shape[0] // base_ref.shape[0]
    for block in range(base_ref.shape[0]):
        for part in range(bias_ref.shape[1] // 128):
            lanes = slice(128 * part, 128 * (part + 1))
            shape = (tokens, 128)
            key_pos = base_ref[block] + lax.broadcasted_iota(jnp.int32, shape, 0)
            inside = (key_pos >= bounds_ref[0:1, lanes]) & (key_pos <= bounds_ref[1:2, lanes])
            bias_ref[pl.ds(block * tokens, tokens), lanes] = jnp.where(inside, 0.0, masked_score)


def attend_kernel(base_ref, bounds_ref, query_ref, key_ref, value_ref, mixed_ref, total_ref, bias_ref):
    @pl.when(pl.program_id(0) == 0)
    def _():
        mask_bias(bias_ref, bounds_ref, base_ref)

    keys = key_ref[...]
    values = value_ref[...]
    for part in range(query_ref.shape[1] // 128):
        lanes = slice(128 * part, 128 * (part + 1))
        queries = query_ref[:, lanes]
        scores = contract(keys, queries, 0, 0) * (1.0 / math.sqrt(HD)) + bias_ref[:, lanes]
        row_max = jnp.max(scores, axis=0, keepdims=True)
        weights = jnp.exp(scores - row_max)
        row_sum = jnp.sum(weights, axis=0, keepdims=True)
        total_ref[0, :, lanes] = row_max + jnp.log(row_sum)
        probs = (weights * (1.0 / row_sum)).astype(bf16)
        mixed_ref[:, lanes] = contract(values, probs, 1, 0).astype(bf16)


def attend_back_kernel(
    base_ref,
    bounds_ref,
    query_ref,
    key_ref,
    value_ref,
    mixed_ref,
    grad_ref,
    total_ref,
    out_ref,
    bias_ref,
    probs_ref,
    slope_ref,
):
    @pl.when(pl.program_id(0) == 0)
    def _():
        mask_bias(bias_ref, bounds_ref, base_ref)

    keys = key_ref[...]
    values = value_ref[...]
    scale = 1.0 / math.sqrt(HD)
    for part in range(query_ref.shape[1] // 128):
        lanes = slice(128 * part, 128 * (part + 1))
        queries = query_ref[:, lanes]
        grads = grad_ref[:, lanes]
        scores = contract(keys, queries, 0, 0) * scale + bias_ref[:, lanes]
        probs = jnp.exp(scores - total_ref[0, :, lanes])
        delta = jnp.sum(grads.astype(f32) * mixed_ref[:, lanes].astype(f32), axis=0, keepdims=True)
        grad_probs = contract(values, grads, 0, 0)
        slope = (probs * (grad_probs - delta) * scale).astype(bf16)
        probs_ref[:, lanes] = probs.astype(bf16)
        slope_ref[:, lanes] = slope
        out_ref[0, :, lanes] = contract(keys, slope, 1, 0).astype(bf16)
    slope = slope_ref[...]
    out_ref[1] = contract(query_ref[...], slope, 1, 1).astype(bf16)
    out_ref[2] = contract(grad_ref[...], probs_ref[...], 1, 1).astype(bf16)


def attend(projected, bounds, bases, heads):
    seq = projected.shape[1]
    row = lambda shift: pl.BlockSpec((HD, seq), lambda h, _: (h + shift, 0))
    return pl.pallas_call(
        attend_kernel,
        grid_spec=pltpu.PrefetchScalarGridSpec(
            num_scalar_prefetch=1,
            grid=(heads,),
            in_specs=[pl.BlockSpec((8, seq), lambda h, _: (0, 0)), row(0), row(heads), row(2 * heads)],
            out_specs=[row(0), pl.BlockSpec((1, 1, seq), lambda h, _: (h, 0, 0))],
            scratch_shapes=[pltpu.VMEM((seq, seq), f32)],
        ),
        out_shape=[
            jax.ShapeDtypeStruct((heads * HD, seq), bf16),
            jax.ShapeDtypeStruct((heads, 1, seq), f32),
        ],
        cost_estimate=pl.CostEstimate(
            flops=4 * heads * seq * seq * HD,
            transcendentals=heads * seq * seq,
            bytes_accessed=8 * heads * HD * seq,
        ),
        name="attend",
    )(bases, bounds, projected, projected, projected)


def attend_back(projected, mixed, grad_mixed, totals, bounds, bases, heads):
    seq = projected.shape[1]
    row = lambda shift: pl.BlockSpec((HD, seq), lambda h, _: (h + shift, 0))
    return pl.pallas_call(
        attend_back_kernel,
        grid_spec=pltpu.PrefetchScalarGridSpec(
            num_scalar_prefetch=1,
            grid=(heads,),
            in_specs=[
                pl.BlockSpec((8, seq), lambda h, _: (0, 0)),
                row(0),
                row(heads),
                row(2 * heads),
                row(0),
                row(0),
                pl.BlockSpec((1, 1, seq), lambda h, _: (h, 0, 0)),
            ],
            out_specs=pl.BlockSpec((3, HD, seq), lambda h, _: (0, h, 0)),
            scratch_shapes=[
                pltpu.VMEM((seq, seq), f32),
                pltpu.VMEM((seq, seq), bf16),
                pltpu.VMEM((seq, seq), bf16),
            ],
        ),
        out_shape=jax.ShapeDtypeStruct((3, heads * HD, seq), bf16),
        cost_estimate=pl.CostEstimate(
            flops=10 * heads * seq * seq * HD,
            transcendentals=heads * seq * seq,
            bytes_accessed=16 * heads * HD * seq,
        ),
        name="attend_back",
    )(bases, bounds, projected, projected, projected, mixed, grad_mixed, totals)


def shards(
    reps,
    size,
    tokens,
    segments,
    cotangent,
    packed_weight,
    output_weight,
    up_weight,
    down_weight,
    first_gain,
    first_shift,
    query_bias,
    value_bias,
    output_bias,
    second_gain,
    second_shift,
    hidden_bias,
    down_bias,
):
    rank = lax.axis_index("grp")
    rep_rank = lax.axis_index("rep")
    own = D // size
    hidden_own = hidden_bias.shape[0]
    hidden_all = hidden_own * size
    count = tokens.shape[1]
    seq = segments.shape[1]

    begins = [own * g // HD for g in range(size)]
    heads = max(-(-own * (g + 1) // HD) - begins[g] for g in range(size))
    begins = [min(b, HEADS - heads) for b in begins]
    width = heads * HD
    offsets = [own * g - HD * b for g, b in enumerate(begins)]
    margin = max(max(offsets), max(width - own - o for o in offsets))
    begin = jnp.minimum(rank * own // HD, HEADS - heads)
    offset = rank * own - HD * begin

    rows_own = tokens[0]
    row_blocks = group_gather(rows_own, size)
    small = jnp.stack(
        [
            first_gain,
            first_shift,
            query_bias,
            value_bias,
            output_bias,
            second_gain,
            second_shift,
            down_bias,
        ]
    )
    small_blocks = group_gather(small, size)
    packed_sets = jnp.stack(
        [
            jnp.concatenate(
                [packed_weight[:, D * t + HD * b : D * t + HD * b + width] for t in range(3)], axis=1
            )
            for b in begins
        ]
    )
    packed_blocks = [
        swap(lax.dynamic_index_in_dim(packed_sets, rank ^ j, 0, keepdims=False), "grp", size, j)
        if j
        else lax.dynamic_index_in_dim(packed_sets, rank, 0, keepdims=False)
        for j in range(size)
    ]
    up_held, packed_blocks = lax.optimization_barrier((up_weight, packed_blocks))
    up_sets = jnp.stack([up_held[:, hidden_own * g : hidden_own * (g + 1)] for g in range(size)])
    up_blocks = [
        swap(lax.dynamic_index_in_dim(up_sets, rank ^ j, 0, keepdims=False), "grp", size, j)
        if j
        else lax.dynamic_index_in_dim(up_sets, rank, 0, keepdims=False)
        for j in range(size)
    ]
    ahead = lax.ppermute(output_weight[own - margin :], "grp", [(i, i + 1) for i in range(size - 1)])
    behind = lax.ppermute(output_weight[:margin], "grp", [(i + 1, i) for i in range(size - 1)])
    grad_held, up_blocks = lax.optimization_barrier((cotangent[0], up_blocks))
    grad_rows = jnp.concatenate(group_gather(grad_held, size))

    vectors = jnp.zeros((size,) + small.shape, bf16)
    for j in range(size):
        vectors = lax.dynamic_update_slice_in_dim(vectors, small_blocks[j][None], rank ^ j, 0)
    vectors = vectors.transpose(1, 0, 2).reshape(small.shape[0], D).astype(f32)
    packed_cols = place_rows(packed_blocks, rank)
    up_cols = place_rows(up_blocks, rank)
    output_wide = lax.dynamic_slice_in_dim(
        jnp.concatenate([ahead, output_weight, behind]), margin - offset, width, 0
    )
    wide_row = jnp.arange(width, dtype=jnp.int32)[:, None]
    wide_mine = (wide_row >= offset) & (wide_row < offset + own)
    output_mine = jnp.where(wide_mine, output_wide, jnp.zeros_like(output_wide))

    segment_ids = segments[0]
    bases = jnp.stack([(rank ^ j) * count for j in range(size)]).astype(jnp.int32)
    relative = lambda whole: jnp.concatenate(
        [lax.dynamic_slice_in_dim(whole, (rank ^ j) * count, count) for j in range(size)]
    )
    position = relative(jnp.arange(seq, dtype=jnp.int32))
    segment_rows = relative(segment_ids)
    doc_begin = jnp.sum((segment_ids[:, None] < segment_rows[None, :]).astype(jnp.int32), axis=0)
    bounds = jnp.zeros((8, seq), jnp.int32).at[0].set(doc_begin).at[1].set(position)

    rows_all = jnp.concatenate(row_blocks).astype(f32)
    normal_a = (norm_rows(rows_all)[0] * vectors[0] + vectors[1]).astype(bf16)
    take = lambda vector: lax.dynamic_slice_in_dim(vector, begin * HD, width)
    packed_bias = jnp.concatenate([take(vectors[2]), jnp.zeros((width,), f32), take(vectors[3])])
    projected = (contract(packed_cols, normal_a, 0, 1) + packed_bias[:, None]).astype(bf16)
    mixed, totals = attend(projected, bounds, bases, heads)
    attn_part = contract(mixed, output_mine, 0, 0)
    rows_float = rows_own.astype(f32)
    residual = rows_float + group_scatter_sum(token_blocks(attn_part, size), size) + vectors[4]
    normed_second, inv_second = norm_rows(residual)
    normal_c_own = (normed_second * vectors[5] + vectors[6]).astype(bf16)
    normal_c = jnp.concatenate(group_gather(normal_c_own, size))
    pre_act = contract(normal_c, up_cols, 1, 0) + hidden_bias.astype(f32)
    gelu_value, gelu_slope = gelu_parts(pre_act)
    hidden = gelu_value.astype(bf16)

    grad_hidden = contract(grad_rows, down_weight, 1, 1)
    grad_pre = (grad_hidden * gelu_slope).astype(bf16)
    grad_c_part = contract(grad_pre, up_cols, 1, 1)
    grad_c = group_scatter_sum(token_blocks(grad_c_part, size), size)
    grad_up = contract(grad_pre, normal_c, 0, 0)
    grad_down = contract(grad_rows, hidden, 0, 0)
    layer_part = contract(hidden, down_weight, 1, 0)
    layer_rows = residual + group_scatter_sum(token_blocks(layer_part, size), size) + vectors[7]

    up_piece = scatter_pieces(grad_up, reps, size, 0)
    down_piece = scatter_natural(grad_down, reps)
    share = reps // size
    route = []
    for r in range(reps):
        row_part, lane_part = piece_of(r, reps, size)
        for g in range(size):
            route.append((r * size + g, (g * share + row_part) * size + lane_part))
    final_up = lax.ppermute(up_piece.astype(bf16), ("rep", "grp"), route).astype(f32).T
    final_down = down_piece.T

    grad_float = cotangent[0].astype(f32)
    grad_resid = grad_float + norm_back(grad_c, normed_second, inv_second, vectors[5])
    grad_attn_own = grad_resid.astype(bf16)
    grad_attn = jnp.concatenate(group_gather(grad_attn_own, size))
    hidden_sums = jnp.zeros((hidden_all,), f32)
    hidden_sums = lax.dynamic_update_slice_in_dim(
        hidden_sums, jnp.sum(grad_pre.astype(f32), axis=0), rank * hidden_own, 0
    )
    early = jnp.concatenate(
        [
            jnp.sum(grad_float, axis=0),
            jnp.sum(grad_attn_own.astype(f32), axis=0),
            jnp.sum(grad_c * normed_second, axis=0),
            jnp.sum(grad_c, axis=0),
            hidden_sums,
        ]
    )
    early = sum_everywhere(early.reshape(-1, 128), reps, size).reshape(-1)

    grad_mixed = contract(output_wide, grad_attn, 1, 1).astype(bf16)
    grad_packed_rows = attend_back(projected, mixed, grad_mixed, totals, bounds, bases, heads)
    grad_mine = lax.dynamic_slice_in_dim(grad_packed_rows, offset, own, 1)
    grad_packed = contract(grad_mine.reshape(3 * own, seq), normal_a, 1, 0).reshape(3, own, D)
    packed_piece = scatter_pieces(grad_packed, reps, size, 1)
    mixed_mine = lax.dynamic_slice_in_dim(mixed, offset, own, 0)
    grad_output = contract(grad_attn, mixed_mine, 0, 1)
    final_output = scatter_natural(grad_output, reps).T

    grad_masked = jnp.where(wide_mine[None], grad_packed_rows, jnp.zeros_like(grad_packed_rows))
    grad_a_part = contract(grad_masked.reshape(3 * width, seq), packed_cols, 0, 1)
    grad_a = group_scatter_sum(token_blocks(grad_a_part, size), size)
    normed_first, inv_first = norm_rows(rows_float)
    grad_in = grad_resid + norm_back(grad_a, normed_first, inv_first, vectors[0])

    def feature_sums(rows):
        return lax.dynamic_update_slice_in_dim(
            jnp.zeros((D,), f32), jnp.sum(rows.astype(f32), axis=1), rank * own, 0
        )

    late = jnp.concatenate(
        [
            jnp.sum(grad_a * normed_first, axis=0),
            jnp.sum(grad_a, axis=0),
            feature_sums(grad_mine[0]),
            feature_sums(grad_mine[2]),
        ]
    )
    late = sum_everywhere(late.reshape(-1, 128), reps, size).reshape(-1)

    kinds = packed_piece.shape[0]
    rounds = match_rounds(reps, kinds)
    table = jnp.array(rounds, jnp.int32)
    unit = rank * share + piece_of(rep_rank, reps, size)[0]
    pieces = packed_piece.astype(bf16)
    origin = [[0] * kinds for _ in range(reps)]
    received = []
    for turn, chosen in enumerate(rounds):
        route = []
        for r in range(reps):
            row_part, lane_part = piece_of(r, reps, size)
            for g in range(size):
                v = g * share + row_part
                where = reps * chosen[v] + v
                origin[where // kinds][where % kinds] = turn
                route.append((r * size + g, (where // kinds) * size + lane_part))
        sent = lax.dynamic_index_in_dim(pieces, table[turn, unit], 0, keepdims=False)
        received.append(lax.ppermute(sent, ("rep", "grp"), route))
    received = jnp.stack(received)
    order = jnp.array(origin, jnp.int32)[rep_rank]
    final_packed = jnp.concatenate(
        [
            lax.dynamic_index_in_dim(received, order[k], 0, keepdims=False)
            for k in range(kinds)
        ]
    ).astype(f32).T

    return (
        layer_rows[None],
        grad_in[None],
        final_packed,
        final_output,
        final_up,
        final_down,
        late[:D],
        late[D : 2 * D],
        late[2 * D : 3 * D],
        late[3 * D :],
        early[D : 2 * D],
        early[2 * D : 3 * D],
        early[3 * D : 4 * D],
        early[4 * D :],
        early[:D],
    )


def solution(mesh):
    in_specs = (
        P("rep", "grp", None),
        P("rep", None),
        P("rep", "grp", None),
        P("grp", None),
        P("grp", None),
        P("grp", None),
        P("grp", None),
    ) + (P("grp"),) * 9
    out_specs = (
        P("rep", "grp", None),
        P("rep", "grp", None),
        P("grp", "rep"),
        P("grp", "rep"),
        P("grp", "rep"),
        P("grp", "rep"),
    ) + (P(),) * 9
    body = functools.partial(shards, mesh.shape["rep"], mesh.shape["grp"])
    return jax.shard_map(body, mesh=mesh, in_specs=in_specs, out_specs=out_specs, check_vma=False)
```

```python
import math

import jax
import jax.numpy as jnp
from jax import lax
from jax.experimental import pallas as pl
from jax.experimental.pallas import tpu as pltpu
from jax.sharding import PartitionSpec as P

D = 1088
HEADS = 17
HD = 64

epsilon = 1e-05
gelu_factor = 0.7978845608028654
masked_score = -1e30
f32 = jnp.float32
bf16 = jnp.bfloat16


def gelu_parts(pre_act):
    inner = gelu_factor * (pre_act + 0.044715 * pre_act * pre_act * pre_act)
    tanh_value = jnp.tanh(inner)
    gelu_value = 0.5 * pre_act * (1.0 + tanh_value)
    gelu_slope = 0.5 * (1.0 + tanh_value) + 0.5 * pre_act * (
        1.0 - tanh_value * tanh_value
    ) * gelu_factor * (1.0 + 3.0 * 0.044715 * pre_act * pre_act)
    return (gelu_value, gelu_slope)


def norm_rows(field):
    row_mean = jnp.mean(field, axis=-1, keepdims=True)
    centered = field - row_mean
    inv_std = lax.rsqrt(jnp.mean(centered * centered, axis=-1, keepdims=True) + epsilon)
    return (centered * inv_std, inv_std)


def norm_back(grad_out, normed, inv_std, gain_row):
    scaled = grad_out * gain_row
    return inv_std * (
        scaled
        - jnp.mean(scaled, axis=-1, keepdims=True)
        - normed * jnp.mean(scaled * normed, axis=-1, keepdims=True)
    )


def contract(left, right, left_dim, right_dim):
    return lax.dot_general(
        left, right, (((left_dim,), (right_dim,)), ((), ())), preferred_element_type=f32
    )


def swap(value, axis, size, bit):
    return lax.ppermute(value, axis, [(i, i ^ bit) for i in range(size)])


def log2(count):
    return count.bit_length() - 1


def relative_order(size):
    order = [0]
    bit = size // 2
    while bit:
        order = order + [o ^ bit for o in order]
        bit //= 2
    return order


def group_gather(value, size):
    bit = size // 2
    while bit:
        value = jnp.concatenate([value, swap(value, "grp", size, bit)])
        bit //= 2
    return value


def group_scatter_sum(value, size):
    bit = 1
    while bit < size:
        half = value.shape[0] // 2
        moved = swap(value[half:].astype(bf16), "grp", size, bit)
        value = value[:half] + moved.astype(f32)
        bit *= 2
    return value


def place_rows(blocks, rank):
    rows = blocks[0].shape[0]
    whole = jnp.zeros((rows * len(blocks),) + blocks[0].shape[1:], blocks[0].dtype)
    for j, block in enumerate(blocks):
        whole = lax.dynamic_update_slice_in_dim(whole, block, (rank ^ j) * rows, 0)
    return whole


def sum_everywhere(vector, reps, size):
    for axis, count in (("grp", size), ("rep", reps)):
        bit = 1
        while bit < count:
            moved = swap(vector, axis, count, bit)
            vector = vector + moved
            bit *= 2
    return vector


def rep_bit(bit):
    return (lax.axis_index("rep") >> bit) & 1


def halve_rows(value, bit, reps, axis):
    mine = rep_bit(bit)
    half = value.shape[axis] // 2
    keep = lax.dynamic_slice_in_dim(value, mine * half, half, axis)
    give = lax.dynamic_slice_in_dim(value, (1 - mine) * half, half, axis).astype(bf16)
    moved = swap(give, "rep", reps, 1 << bit)
    return keep + moved.astype(f32)


def halve_lanes(value, bit, reps):
    mine = rep_bit(bit) == 1
    half = value.shape[-1] // 2
    low, high = value[..., :half], value[..., half:]
    give = jnp.where(mine, low, high).astype(bf16)
    moved = swap(give, "rep", reps, 1 << bit)
    return jnp.where(mine, high, low) + moved.astype(f32)


def natural_rows(value, reps):
    return value.reshape((2,) * log2(reps) + (value.shape[0] // reps,) + value.shape[1:])


def natural_step(value, bit, bits_left, reps):
    axis = len(bits_left) - 1 - sorted(bits_left).index(bit)
    return lax.squeeze(halve_rows(value, bit, reps, axis), (axis,))


def quad_step(value, axis, reps, size):
    low = lax.axis_index("rep") & (size - 1)
    pick = lambda o: lax.dynamic_index_in_dim(value, low ^ o, axis, keepdims=False)
    gives = [pick(o).astype(bf16) for o in range(1, size)]
    total = pick(0)
    moved = [swap(give, "rep", reps, o + 1) for o, give in enumerate(gives)]
    for part in moved:
        total = total + part.astype(f32)
    return total


def piece_of(rep, reps, size):
    row_part = 0
    for bit in range(log2(size), log2(reps)):
        row_part = 2 * row_part + ((rep >> bit) & 1)
    return row_part, rep & (size - 1)


def match_rounds(reps, kinds):
    left = {v: set(range(kinds)) for v in range(reps)}
    rounds = []
    for _ in range(kinds):
        owner = {}

        def place(v, seen):
            for kind in sorted(left[v]):
                target = (reps * kind + v) // kinds
                if target in seen:
                    continue
                seen.add(target)
                if target not in owner or place(owner[target][0], seen):
                    owner[target] = (v, kind)
                    return True
            return False

        for v in range(reps):
            place(v, set())
        chosen = [0] * reps
        for v, kind in owner.values():
            chosen[v] = kind
            left[v].discard(kind)
        rounds.append(chosen)
    return rounds


def mask_bias(bias_ref, bounds_ref, base_ref):
    tokens = bias_ref.shape[0] // base_ref.shape[0]
    for block in range(base_ref.shape[0]):
        for part in range(bias_ref.shape[1] // 128):
            lanes = slice(128 * part, 128 * (part + 1))
            shape = (tokens, 128)
            key_pos = base_ref[block] + lax.broadcasted_iota(jnp.int32, shape, 0)
            inside = (key_pos >= bounds_ref[0:1, lanes]) & (key_pos <= bounds_ref[1:2, lanes])
            bias_ref[pl.ds(block * tokens, tokens), lanes] = jnp.where(inside, 0.0, masked_score)


def attend_kernel(base_ref, bounds_ref, query_ref, key_ref, value_ref, mixed_ref, total_ref, bias_ref):
    @pl.when(pl.program_id(0) == 0)
    def _():
        mask_bias(bias_ref, bounds_ref, base_ref)

    keys = key_ref[...]
    values = value_ref[...]
    for part in range(query_ref.shape[1] // 128):
        lanes = slice(128 * part, 128 * (part + 1))
        queries = query_ref[:, lanes]
        scores = contract(keys, queries, 0, 0) * (1.0 / math.sqrt(HD)) + bias_ref[:, lanes]
        row_max = jnp.max(scores, axis=0, keepdims=True)
        weights = jnp.exp(scores - row_max)
        row_sum = jnp.sum(weights, axis=0, keepdims=True)
        total_ref[0, :, lanes] = row_max + jnp.log(row_sum)
        probs = (weights * (1.0 / row_sum)).astype(bf16)
        mixed_ref[:, lanes] = contract(values, probs, 1, 0).astype(bf16)


def attend_back_kernel(
    base_ref,
    bounds_ref,
    query_ref,
    key_ref,
    value_ref,
    mixed_ref,
    grad_ref,
    total_ref,
    out_ref,
    bias_ref,
    probs_ref,
    slope_ref,
):
    @pl.when(pl.program_id(0) == 0)
    def _():
        mask_bias(bias_ref, bounds_ref, base_ref)

    keys = key_ref[...]
    values = value_ref[...]
    scale = 1.0 / math.sqrt(HD)
    for part in range(query_ref.shape[1] // 128):
        lanes = slice(128 * part, 128 * (part + 1))
        queries = query_ref[:, lanes]
        grads = grad_ref[:, lanes]
        scores = contract(keys, queries, 0, 0) * scale + bias_ref[:, lanes]
        probs = jnp.exp(scores - total_ref[0, :, lanes])
        delta = jnp.sum(grads.astype(f32) * mixed_ref[:, lanes].astype(f32), axis=0, keepdims=True)
        grad_probs = contract(values, grads, 0, 0)
        slope = (probs * (grad_probs - delta) * scale).astype(bf16)
        probs_ref[:, lanes] = probs.astype(bf16)
        slope_ref[:, lanes] = slope
        out_ref[0, :, lanes] = contract(keys, slope, 1, 0).astype(bf16)
    slope = slope_ref[...]
    out_ref[1] = contract(query_ref[...], slope, 1, 1).astype(bf16)
    out_ref[2] = contract(grad_ref[...], probs_ref[...], 1, 1).astype(bf16)


def attend(projected, bounds, bases, heads):
    seq = projected.shape[1]
    row = lambda shift: pl.BlockSpec((HD, seq), lambda h, _: (h + shift, 0))
    return pl.pallas_call(
        attend_kernel,
        grid_spec=pltpu.PrefetchScalarGridSpec(
            num_scalar_prefetch=1,
            grid=(heads,),
            in_specs=[pl.BlockSpec((8, seq), lambda h, _: (0, 0)), row(0), row(heads), row(2 * heads)],
            out_specs=[row(0), pl.BlockSpec((1, 1, seq), lambda h, _: (h, 0, 0))],
            scratch_shapes=[pltpu.VMEM((seq, seq), f32)],
        ),
        out_shape=[
            jax.ShapeDtypeStruct((heads * HD, seq), bf16),
            jax.ShapeDtypeStruct((heads, 1, seq), f32),
        ],
        cost_estimate=pl.CostEstimate(
            flops=4 * heads * seq * seq * HD,
            transcendentals=heads * seq * seq,
            bytes_accessed=8 * heads * HD * seq,
        ),
        name="attend",
    )(bases, bounds, projected, projected, projected)


def attend_back(projected, mixed, grad_mixed, totals, bounds, bases, heads):
    seq = projected.shape[1]
    row = lambda shift: pl.BlockSpec((HD, seq), lambda h, _: (h + shift, 0))
    return pl.pallas_call(
        attend_back_kernel,
        grid_spec=pltpu.PrefetchScalarGridSpec(
            num_scalar_prefetch=1,
            grid=(heads,),
            in_specs=[
                pl.BlockSpec((8, seq), lambda h, _: (0, 0)),
                row(0),
                row(heads),
                row(2 * heads),
                row(0),
                row(0),
                pl.BlockSpec((1, 1, seq), lambda h, _: (h, 0, 0)),
            ],
            out_specs=pl.BlockSpec((3, HD, seq), lambda h, _: (0, h, 0)),
            scratch_shapes=[
                pltpu.VMEM((seq, seq), f32),
                pltpu.VMEM((seq, seq), bf16),
                pltpu.VMEM((seq, seq), bf16),
            ],
        ),
        out_shape=jax.ShapeDtypeStruct((3, heads * HD, seq), bf16),
        cost_estimate=pl.CostEstimate(
            flops=10 * heads * seq * seq * HD,
            transcendentals=heads * seq * seq,
            bytes_accessed=16 * heads * HD * seq,
        ),
        name="attend_back",
    )(bases, bounds, projected, projected, projected, mixed, grad_mixed, totals)


def shards(
    reps,
    size,
    tokens,
    segments,
    cotangent,
    packed_weight,
    output_weight,
    up_weight,
    down_weight,
    first_gain,
    first_shift,
    query_bias,
    value_bias,
    output_bias,
    second_gain,
    second_shift,
    hidden_bias,
    down_bias,
):
    rank = lax.axis_index("grp")
    rep_rank = lax.axis_index("rep")
    own = D // size
    hidden_own = hidden_bias.shape[0]
    hidden_all = hidden_own * size
    count = tokens.shape[1]
    seq = segments.shape[1]

    begins = [own * g // HD for g in range(size)]
    heads = max(-(-own * (g + 1) // HD) - begins[g] for g in range(size))
    begins = [min(b, HEADS - heads) for b in begins]
    width = heads * HD
    offsets = [own * g - HD * b for g, b in enumerate(begins)]
    margin = max(max(offsets), max(width - own - o for o in offsets))
    begin = jnp.minimum(rank * own // HD, HEADS - heads)
    offset = rank * own - HD * begin

    order = relative_order(size)
    rows_own = tokens[0]
    rows_all = group_gather(rows_own, size)
    starts = [[D * t + HD * b for t in range(3)] for b in begins]
    packed_sets = jnp.stack(
        [jnp.concatenate([packed_weight[:, o : o + width] for o in at], axis=1) for at in starts]
    )
    packed_give = [
        lax.dynamic_index_in_dim(packed_sets, rank ^ j, 0, keepdims=False) for j in range(size)
    ]
    packed_blocks = [packed_give[0]] + [None] * (size - 1)
    for j in reversed(range(1, size)):
        packed_blocks[j] = swap(packed_give[j], "grp", size, j)
    shorts = (
        first_gain,
        first_shift,
        query_bias,
        value_bias,
        output_bias,
        second_gain,
        second_shift,
        down_bias,
    )
    shorts, packed_give = lax.optimization_barrier((shorts, packed_give))
    small = jnp.stack(shorts)
    kinds = small.shape[0]
    small = group_gather(small, size).reshape(size, kinds, own)
    packed_cols = place_rows(packed_blocks, rank)

    up_held, cot_held, out_held, packed_blocks = lax.optimization_barrier(
        (up_weight, cotangent[0], output_weight, packed_blocks)
    )
    up_sets = jnp.stack([up_held[:, hidden_own * g : hidden_own * (g + 1)] for g in range(size)])
    up_blocks, cot_blocks = [None] * size, [None] * size
    up_blocks[0] = lax.dynamic_index_in_dim(up_sets, rank, 0, keepdims=False)
    cot_blocks[0] = cot_held
    ahead = jnp.zeros((margin, D), bf16)
    behind = jnp.zeros((margin, D), bf16)
    for j in reversed(range(1, size)):
        other = rank ^ j
        edge = jnp.where(other > rank, out_held[own - margin :], out_held[:margin])
        give = jnp.concatenate(
            [lax.dynamic_index_in_dim(up_sets, other, 0, keepdims=False), cot_held, edge]
        )
        got = swap(give, "grp", size, j)
        up_blocks[j], cot_blocks[j], edge = got[:own], got[own : own + count], got[own + count :]
        ahead = jnp.where(other == rank - 1, edge, ahead)
        behind = jnp.where(other == rank + 1, edge, behind)
    grad_rows = jnp.concatenate([cot_blocks[o] for o in order])
    vectors = jnp.zeros((size, kinds, own), bf16)
    for i, o in enumerate(order):
        vectors = lax.dynamic_update_slice_in_dim(vectors, small[i][None], rank ^ o, 0)
    vectors = vectors.transpose(1, 0, 2).reshape(kinds, D).astype(f32)
    up_cols = place_rows(up_blocks, rank)
    output_wide = lax.dynamic_slice_in_dim(
        jnp.concatenate([ahead, output_weight, behind]), margin - offset, width, 0
    )
    wide_row = jnp.arange(width, dtype=jnp.int32)[:, None]
    wide_mine = (wide_row >= offset) & (wide_row < offset + own)
    output_mine = jnp.where(wide_mine, output_wide, jnp.zeros_like(output_wide))

    segment_ids = segments[0]
    bases = jnp.stack([(rank ^ o) * count for o in order]).astype(jnp.int32)
    relative = lambda whole: jnp.concatenate(
        [lax.dynamic_slice_in_dim(whole, (rank ^ o) * count, count) for o in order]
    )
    position = relative(jnp.arange(seq, dtype=jnp.int32))
    segment_rows = relative(segment_ids)
    doc_begin = jnp.sum((segment_ids[:, None] < segment_rows[None, :]).astype(jnp.int32), axis=0)
    bounds = jnp.zeros((8, seq), jnp.int32).at[0].set(doc_begin).at[1].set(position)

    normal_a = (norm_rows(rows_all.astype(f32))[0] * vectors[0] + vectors[1]).astype(bf16)
    take = lambda vector: lax.dynamic_slice_in_dim(vector, begin * HD, width)
    packed_bias = jnp.concatenate([take(vectors[2]), jnp.zeros((width,), f32), take(vectors[3])])
    projected = (contract(packed_cols, normal_a, 0, 1) + packed_bias[:, None]).astype(bf16)
    mixed, totals = attend(projected, bounds, bases, heads)
    attn_part = contract(mixed, output_mine, 0, 0)
    rows_float = rows_own.astype(f32)
    residual = rows_float + group_scatter_sum(attn_part, size) + vectors[4]
    normed_second, inv_second = norm_rows(residual)
    normal_c_own = (normed_second * vectors[5] + vectors[6]).astype(bf16)
    normal_c = group_gather(normal_c_own, size)
    pre_act = contract(normal_c, up_cols, 1, 0) + hidden_bias.astype(f32)
    gelu_value, gelu_slope = gelu_parts(pre_act)
    hidden = gelu_value.astype(bf16)

    grad_hidden = contract(grad_rows, down_weight, 1, 1)
    grad_pre = (grad_hidden * gelu_slope).astype(bf16)
    grad_c_part = contract(grad_pre, up_cols, 1, 1)
    grad_c = group_scatter_sum(grad_c_part, size)
    grad_down = contract(grad_rows, hidden, 0, 0)
    grad_up = contract(normal_c, grad_pre, 0, 0)
    layer_part = contract(hidden, down_weight, 1, 0)

    left = list(range(log2(reps)))
    down_piece = natural_rows(grad_down, reps)
    while left:
        down_piece = natural_step(down_piece, left[0], left, reps)
        left = left[1:]
    final_down = down_piece.T
    up_piece = grad_up
    for step, bit in enumerate(list(reversed(range(log2(size)))) + list(range(log2(size), log2(reps)))):
        if step < log2(size):
            up_piece = halve_rows(up_piece, bit, reps, 0)
        else:
            up_piece = halve_lanes(up_piece, bit, reps)
    share = reps // size
    route = []
    for r in range(reps):
        row_part, lane_part = piece_of(r, reps, size)
        for g in range(size):
            route.append((r * size + g, (g * share + row_part) * size + lane_part))
    final_up = lax.ppermute(up_piece.astype(bf16), ("rep", "grp"), route).astype(f32)

    grad_float = cotangent[0].astype(f32)
    grad_resid = grad_float + norm_back(grad_c, normed_second, inv_second, vectors[5])
    grad_attn_own = grad_resid.astype(bf16)
    grad_attn = group_gather(grad_attn_own, size)

    grad_mixed = contract(output_wide, grad_attn, 1, 1).astype(bf16)
    grad_packed_rows = attend_back(projected, mixed, grad_mixed, totals, bounds, bases, heads)
    grad_mine = lax.dynamic_slice_in_dim(grad_packed_rows, offset, own, 1)
    grad_packed = contract(normal_a, grad_mine.reshape(3 * own, seq), 0, 1)
    piece = quad_step(grad_packed.reshape(size, own, 3 * own), 0, reps, size)
    piece = jnp.stack([piece[:, own * t : own * (t + 1)] for t in range(3)])
    for bit in range(log2(size), log2(reps)):
        piece = halve_lanes(piece, bit, reps)
    mixed_mine = lax.dynamic_slice_in_dim(mixed, offset, own, 0)
    grad_output = contract(grad_attn, mixed_mine, 0, 1)
    out_piece = quad_step(grad_output.reshape(share, size, D // reps, own), 1, reps, size)
    for bit in reversed(range(log2(size), log2(reps))):
        out_piece = halve_rows(out_piece, bit, reps, 0)
    final_output = out_piece.reshape(D // reps, own).T

    grad_masked = jnp.where(wide_mine[None], grad_packed_rows, jnp.zeros_like(grad_packed_rows))
    grad_a_part = contract(grad_masked.reshape(3 * width, seq), packed_cols, 0, 1)
    grad_a = group_scatter_sum(grad_a_part, size)
    layer_rows = residual + group_scatter_sum(layer_part, size) + vectors[7]
    normed_first, inv_first = norm_rows(rows_float)
    grad_in = grad_resid + norm_back(grad_a, normed_first, inv_first, vectors[0])

    def spread(values, length):
        return lax.dynamic_update_slice_in_dim(
            jnp.zeros((length,), f32), values, rank * values.shape[0], 0
        )

    sums = jnp.concatenate(
        [
            jnp.sum(grad_a * normed_first, axis=0),
            jnp.sum(grad_a, axis=0),
            spread(jnp.sum(grad_mine[0].astype(f32), axis=1), D),
            spread(jnp.sum(grad_mine[2].astype(f32), axis=1), D),
            jnp.sum(grad_attn_own.astype(f32), axis=0),
            jnp.sum(grad_c * normed_second, axis=0),
            jnp.sum(grad_c, axis=0),
            spread(jnp.sum(grad_pre.astype(f32), axis=0), hidden_all),
            jnp.sum(grad_float, axis=0),
        ]
    )
    sums = sum_everywhere(sums.reshape(-1, 128), reps, size).reshape(-1)

    rounds = match_rounds(reps, 3)
    table = jnp.array(rounds, jnp.int32)
    unit = rank * share + piece_of(rep_rank, reps, size)[0]
    pieces = piece.astype(bf16)
    origin = [[0] * 3 for _ in range(reps)]
    received = []
    for turn, chosen in enumerate(rounds):
        route = []
        for r in range(reps):
            row_part, lane_part = piece_of(r, reps, size)
            for g in range(size):
                v = g * share + row_part
                where = reps * chosen[v] + v
                origin[where // 3][where % 3] = turn
                route.append((r * size + g, (where // 3) * size + lane_part))
        sent = lax.dynamic_index_in_dim(pieces, table[turn, unit], 0, keepdims=False)
        received.append(lax.ppermute(sent, ("rep", "grp"), route))
    received = jnp.stack(received)
    owner = jnp.array(origin, jnp.int32)[rep_rank]
    final_packed = jnp.concatenate(
        [lax.dynamic_index_in_dim(received, owner[k], 0, keepdims=False) for k in range(3)], axis=1
    ).astype(f32)

    ends = [D, 2 * D, 3 * D, 4 * D, 5 * D, 6 * D, 7 * D, 7 * D + hidden_all]
    return (
        layer_rows[None],
        grad_in[None],
        final_packed,
        final_output,
        final_up,
        final_down,
        *jnp.split(sums, ends),
    )


def solution(mesh):
    in_specs = (
        P("rep", "grp", None),
        P("rep", None),
        P("rep", "grp", None),
        P("grp", None),
        P("grp", None),
        P("grp", None),
        P("grp", None),
    ) + (P("grp"),) * 9
    out_specs = (
        P("rep", "grp", None),
        P("rep", "grp", None),
        P("grp", "rep"),
        P("grp", "rep"),
        P("grp", "rep"),
        P("grp", "rep"),
    ) + (P(),) * 9

    def body(*args):
        return shards(mesh.shape["rep"], mesh.shape["grp"], *args)

    return jax.shard_map(body, mesh=mesh, in_specs=in_specs, out_specs=out_specs, check_vma=False)
```

```python
import math

import jax
import jax.numpy as jnp
from jax import lax
from jax.experimental import pallas as pl
from jax.experimental.pallas import tpu as pltpu
from jax.sharding import PartitionSpec as P

D = 1088
HEADS = 17
HD = 64

epsilon = 1e-05
gelu_factor = 0.7978845608028654
masked_score = -1e30
f32 = jnp.float32
bf16 = jnp.bfloat16


def gelu_parts(pre_act):
    inner = gelu_factor * (pre_act + 0.044715 * pre_act * pre_act * pre_act)
    tanh_value = jnp.tanh(inner)
    gelu_value = 0.5 * pre_act * (1.0 + tanh_value)
    gelu_slope = 0.5 * (1.0 + tanh_value) + 0.5 * pre_act * (
        1.0 - tanh_value * tanh_value
    ) * gelu_factor * (1.0 + 3.0 * 0.044715 * pre_act * pre_act)
    return (gelu_value, gelu_slope)


def norm_rows(field):
    row_mean = jnp.mean(field, axis=-1, keepdims=True)
    centered = field - row_mean
    inv_std = lax.rsqrt(jnp.mean(centered * centered, axis=-1, keepdims=True) + epsilon)
    return (centered * inv_std, inv_std)


def norm_back(grad_out, normed, inv_std, gain_row):
    scaled = grad_out * gain_row
    return inv_std * (
        scaled
        - jnp.mean(scaled, axis=-1, keepdims=True)
        - normed * jnp.mean(scaled * normed, axis=-1, keepdims=True)
    )


def contract(left, right, left_dim, right_dim):
    return lax.dot_general(
        left, right, (((left_dim,), (right_dim,)), ((), ())), preferred_element_type=f32
    )


def swap(value, axis, size, bit):
    return lax.ppermute(value, axis, [(i, i ^ bit) for i in range(size)])


def starts_at(value, start, axis):
    starts = [0] * value.ndim
    starts[axis] = start
    return starts


def cut(value, start, length, axis):
    sizes = list(value.shape)
    sizes[axis] = length
    starts = starts_at(value, start, axis)
    return lax.dynamic_slice(value, starts, sizes, allow_negative_indices=False)


def pick(value, index, axis):
    return lax.squeeze(cut(value, index, 1, axis), (axis,))


def put(whole, part, start, axis):
    starts = starts_at(whole, start, axis)
    return lax.dynamic_update_slice(whole, part, starts, allow_negative_indices=False)


def log2(count):
    return count.bit_length() - 1


def relative_order(size):
    order = [0]
    bit = size // 2
    while bit:
        order = order + [o ^ bit for o in order]
        bit //= 2
    return order


def group_gather(value, size):
    bit = size // 2
    while bit:
        value = jnp.concatenate([value, swap(value, "grp", size, bit)])
        bit //= 2
    return value


def group_scatter_sum(value, size):
    bit = 1
    while bit < size:
        half = value.shape[0] // 2
        moved = swap(value[half:].astype(bf16), "grp", size, bit)
        value = value[:half] + moved.astype(f32)
        bit *= 2
    return value


def place_kernel(rank_ref, *refs):
    out_ref = refs[-1]
    for j, ref in enumerate(refs[:-1]):
        rows = ref.shape[0]
        out_ref[pl.ds(pl.multiple_of((rank_ref[0] ^ j) * rows, 16), rows), :] = ref[...]


def place_rows(blocks, rank):
    rows, cols = blocks[0].shape
    size = len(blocks)
    if rows % 16:
        whole = jnp.zeros((rows * size, cols), blocks[0].dtype)
        for j, block in enumerate(blocks):
            whole = put(whole, block, (rank ^ j) * rows, 0)
        return whole
    return pl.pallas_call(
        place_kernel,
        grid_spec=pltpu.PrefetchScalarGridSpec(
            num_scalar_prefetch=1,
            grid=(1,),
            in_specs=[pl.BlockSpec((rows, cols), lambda i, _: (0, 0))] * size,
            out_specs=pl.BlockSpec((rows * size, cols), lambda i, _: (0, 0)),
        ),
        out_shape=jax.ShapeDtypeStruct((rows * size, cols), blocks[0].dtype),
        cost_estimate=pl.CostEstimate(
            flops=0, transcendentals=0, bytes_accessed=4 * rows * size * cols
        ),
    )(rank.reshape(1), *blocks)


def first_head(rank, size):
    return lax.div(rank * (D // size), HD)


def pack_kernel(width, rank_ref, source_ref, *out_refs):
    for j, out_ref in enumerate(out_refs):
        begin = first_head(rank_ref[0] ^ j, len(out_refs)) * HD
        parts = []
        for t in range(3):
            shift = D * t % 128
            start = pl.multiple_of(begin + (D * t - shift), 128)
            parts.append(source_ref[:, pl.ds(start, shift + width)][:, shift:])
        out_ref[...] = jnp.concatenate(parts, axis=1)


def pack_columns(weight, begins, width, rank, size):
    starts = [min(b * HD, D - width) for b in begins]
    if any(start % 128 or start != b * HD for start, b in zip(starts, begins)):
        sets = jnp.stack(
            [
                jnp.concatenate([weight[:, D * t + o : D * t + o + width] for t in range(3)], axis=1)
                for o in starts
            ]
        )
        return [pick(sets, rank ^ j, 0) for j in range(size)]
    rows = weight.shape[0]
    return pl.pallas_call(
        lambda *refs: pack_kernel(width, *refs),
        grid_spec=pltpu.PrefetchScalarGridSpec(
            num_scalar_prefetch=1,
            grid=(1,),
            in_specs=[pl.BlockSpec(weight.shape, lambda i, _: (0, 0))],
            out_specs=[pl.BlockSpec((rows, 3 * width), lambda i, _: (0, 0))] * size,
        ),
        out_shape=[jax.ShapeDtypeStruct((rows, 3 * width), weight.dtype)] * size,
        cost_estimate=pl.CostEstimate(
            flops=0, transcendentals=0, bytes_accessed=14 * rows * width * size
        ),
        name="pack_columns",
    )(rank.reshape(1), weight)


def tie(values, deps):
    return lax.optimization_barrier((values, deps))[0]


def sum_over(vector, axis, count):
    bit = 1
    while bit < count:
        moved = swap(vector, axis, count, bit)
        vector = vector + moved
        bit *= 2
    return vector


def rep_bit(bit):
    return (lax.axis_index("rep") >> bit) & 1


def add_parts(parts, dtype):
    total = parts[0].astype(f32)
    for part in parts[1:]:
        total = total + part.astype(f32)
    return total.astype(dtype)


def halve_rows(value, bit, reps, axis):
    mine = rep_bit(bit)
    half = value.shape[axis] // 2
    keep = cut(value, mine * half, half, axis)
    give = cut(value, (1 - mine) * half, half, axis).astype(bf16)
    return keep, swap(give, "rep", reps, 1 << bit)


def halve_lanes(value, bit, reps):
    mine = rep_bit(bit) == 1
    half = value.shape[-1] // 2
    low, high = value[..., :half], value[..., half:]
    give = jnp.where(mine, low, high).astype(bf16)
    return jnp.where(mine, high, low), swap(give, "rep", reps, 1 << bit)


def natural_rows(value, reps):
    return value.reshape((2,) * log2(reps) + (value.shape[0] // reps,) + value.shape[1:])


def quad_step(value, axis, reps, size):
    low = lax.axis_index("rep") & (size - 1)
    block = lambda o: pick(value, low ^ o, axis)
    gives = [block(o).astype(bf16) for o in range(1, size)]
    return [block(0)] + [swap(give, "rep", reps, o + 1) for o, give in enumerate(gives)]


def piece_of(rep, reps, size):
    row_part = 0
    for bit in range(log2(size), log2(reps)):
        row_part = 2 * row_part + ((rep >> bit) & 1)
    return row_part, rep & (size - 1)


def match_rounds(reps, kinds):
    left = {v: set(range(kinds)) for v in range(reps)}
    rounds = []
    for _ in range(kinds):
        owner = {}

        def place(v, seen):
            for kind in sorted(left[v]):
                target = (reps * kind + v) // kinds
                if target in seen:
                    continue
                seen.add(target)
                if target not in owner or place(owner[target][0], seen):
                    owner[target] = (v, kind)
                    return True
            return False

        for v in range(reps):
            place(v, set())
        chosen = [0] * reps
        for v, kind in owner.values():
            chosen[v] = kind
            left[v].discard(kind)
        rounds.append(chosen)
    return rounds


def mask_bias(bias_ref, bounds_ref, rank_ref, blocks):
    order = relative_order(blocks)
    tokens = bias_ref.shape[0] // blocks
    for block in range(blocks):
        for part in range(bias_ref.shape[1] // 128):
            lanes = slice(128 * part, 128 * (part + 1))
            shape = (tokens, 128)
            key_pos = (rank_ref[0] ^ order[block]) * tokens + lax.broadcasted_iota(jnp.int32, shape, 0)
            inside = (key_pos >= bounds_ref[0:1, lanes]) & (key_pos <= bounds_ref[1:2, lanes])
            bias_ref[pl.ds(block * tokens, tokens), lanes] = jnp.where(inside, 0.0, masked_score)


def attend_kernel(blocks, rank_ref, bounds_ref, query_ref, key_ref, value_ref, mixed_ref, total_ref, bias_ref):
    @pl.when(pl.program_id(0) == 0)
    def _():
        mask_bias(bias_ref, bounds_ref, rank_ref, blocks)

    keys = key_ref[...]
    values = value_ref[...]
    for part in range(query_ref.shape[1] // 128):
        lanes = slice(128 * part, 128 * (part + 1))
        queries = query_ref[:, lanes]
        scores = contract(keys, queries, 0, 0) * (1.0 / math.sqrt(HD)) + bias_ref[:, lanes]
        row_max = jnp.max(scores, axis=0, keepdims=True)
        weights = jnp.exp(scores - row_max)
        row_sum = jnp.sum(weights, axis=0, keepdims=True)
        total_ref[0, :, lanes] = row_max + jnp.log(row_sum)
        probs = (weights * (1.0 / row_sum)).astype(bf16)
        mixed_ref[:, lanes] = contract(values, probs, 1, 0).astype(bf16)


def attend_back_kernel(
    blocks,
    rank_ref,
    bounds_ref,
    query_ref,
    key_ref,
    value_ref,
    mixed_ref,
    grad_ref,
    total_ref,
    out_ref,
    bias_ref,
    probs_ref,
    slope_ref,
):
    @pl.when(pl.program_id(0) == 0)
    def _():
        mask_bias(bias_ref, bounds_ref, rank_ref, blocks)

    keys = key_ref[...]
    values = value_ref[...]
    scale = 1.0 / math.sqrt(HD)
    for part in range(query_ref.shape[1] // 128):
        lanes = slice(128 * part, 128 * (part + 1))
        queries = query_ref[:, lanes]
        grads = grad_ref[:, lanes]
        scores = contract(keys, queries, 0, 0) * scale + bias_ref[:, lanes]
        probs = jnp.exp(scores - total_ref[0, :, lanes])
        delta = jnp.sum(grads.astype(f32) * mixed_ref[:, lanes].astype(f32), axis=0, keepdims=True)
        grad_probs = contract(values, grads, 0, 0)
        slope = (probs * (grad_probs - delta) * scale).astype(bf16)
        probs_ref[:, lanes] = probs.astype(bf16)
        slope_ref[:, lanes] = slope
        out_ref[0, :, lanes] = contract(keys, slope, 1, 0).astype(bf16)
    slope = slope_ref[...]
    out_ref[1] = contract(query_ref[...], slope, 1, 1).astype(bf16)
    out_ref[2] = contract(grad_ref[...], probs_ref[...], 1, 1).astype(bf16)


def attend(projected, bounds, rank, blocks, heads):
    seq = projected.shape[1]
    row = lambda shift: pl.BlockSpec((HD, seq), lambda h, _: (h + shift, 0))
    return pl.pallas_call(
        lambda *refs: attend_kernel(blocks, *refs),
        grid_spec=pltpu.PrefetchScalarGridSpec(
            num_scalar_prefetch=1,
            grid=(heads,),
            in_specs=[pl.BlockSpec((8, seq), lambda h, _: (0, 0)), row(0), row(heads), row(2 * heads)],
            out_specs=[row(0), pl.BlockSpec((1, 1, seq), lambda h, _: (h, 0, 0))],
            scratch_shapes=[pltpu.VMEM((seq, seq), f32)],
        ),
        out_shape=[
            jax.ShapeDtypeStruct((heads * HD, seq), bf16),
            jax.ShapeDtypeStruct((heads, 1, seq), f32),
        ],
        cost_estimate=pl.CostEstimate(
            flops=4 * heads * seq * seq * HD,
            transcendentals=heads * seq * seq,
            bytes_accessed=8 * heads * HD * seq,
        ),
        name="attend",
    )(rank.reshape(1), bounds, projected, projected, projected)


def attend_back(projected, mixed, grad_mixed, totals, bounds, rank, blocks, heads):
    seq = projected.shape[1]
    row = lambda shift: pl.BlockSpec((HD, seq), lambda h, _: (h + shift, 0))
    return pl.pallas_call(
        lambda *refs: attend_back_kernel(blocks, *refs),
        grid_spec=pltpu.PrefetchScalarGridSpec(
            num_scalar_prefetch=1,
            grid=(heads,),
            in_specs=[
                pl.BlockSpec((8, seq), lambda h, _: (0, 0)),
                row(0),
                row(heads),
                row(2 * heads),
                row(0),
                row(0),
                pl.BlockSpec((1, 1, seq), lambda h, _: (h, 0, 0)),
            ],
            out_specs=pl.BlockSpec((3, HD, seq), lambda h, _: (0, h, 0)),
            scratch_shapes=[
                pltpu.VMEM((seq, seq), f32),
                pltpu.VMEM((seq, seq), bf16),
                pltpu.VMEM((seq, seq), bf16),
            ],
        ),
        out_shape=jax.ShapeDtypeStruct((3, heads * HD, seq), bf16),
        cost_estimate=pl.CostEstimate(
            flops=10 * heads * seq * seq * HD,
            transcendentals=heads * seq * seq,
            bytes_accessed=16 * heads * HD * seq,
        ),
        name="attend_back",
    )(rank.reshape(1), bounds, projected, projected, projected, mixed, grad_mixed, totals)


def shards(
    reps,
    size,
    tokens,
    segments,
    cotangent,
    packed_weight,
    output_weight,
    up_weight,
    down_weight,
    first_gain,
    first_shift,
    query_bias,
    value_bias,
    output_bias,
    second_gain,
    second_shift,
    hidden_bias,
    down_bias,
):
    rank = lax.axis_index("grp")
    rep_rank = lax.axis_index("rep")
    own = D // size
    hidden_own = hidden_bias.shape[0]
    hidden_all = hidden_own * size
    count = tokens.shape[1]
    seq = segments.shape[1]

    begins = [own * g // HD for g in range(size)]
    heads = max(-(-own * (g + 1) // HD) - begins[g] for g in range(size))
    width = heads * HD
    offsets = [own * g - HD * min(b, HEADS - heads) for g, b in enumerate(begins)]
    margin = max(max(offsets), max(width - own - o for o in offsets))
    begin = first_head(rank, size)
    if begins[-1] * HD > D - width:
        begin = jnp.minimum(begin, HEADS - heads)
    offset = rank * own - HD * begin

    order = relative_order(size)
    rows_own = tokens[0]
    rows_all = group_gather(rows_own, size)
    packed_give = pack_columns(packed_weight, begins, width, rank, size)
    packed_blocks = [packed_give[0]] + [None] * (size - 1)
    for j in reversed(range(1, size)):
        packed_blocks[j] = swap(packed_give[j], "grp", size, j)
    shorts = (
        first_gain,
        first_shift,
        query_bias,
        value_bias,
        output_bias,
        second_gain,
        second_shift,
        down_bias,
    )
    small = jnp.stack(tie(shorts, packed_give))
    kinds = small.shape[0]
    small = group_gather(small, size).reshape(size, kinds, own)
    vectors = jnp.zeros((size, kinds, own), bf16)
    for i, o in enumerate(order):
        vectors = put(vectors, small[i][None], rank ^ o, 0)
    vectors = vectors.transpose(1, 0, 2).reshape(kinds, D).astype(f32)
    packed_cols = place_rows(packed_blocks, rank)

    up_sets = jnp.stack([up_weight[:, hidden_own * g : hidden_own * (g + 1)] for g in range(size)])
    up_give = [pick(up_sets, rank ^ j, 0) for j in range(size)]
    moving = [up_give[j] for j in range(1, size)]
    moving, cot_held, packed_cols = lax.optimization_barrier((moving, cotangent[0], packed_cols))
    up_blocks = [up_give[0]] + [None] * (size - 1)
    for j in reversed(range(1, size)):
        up_blocks[j] = swap(moving[j - 1], "grp", size, j)
    up_cols = place_rows(up_blocks, rank)
    edge_low, edge_high = tie(
        (output_weight[:margin], output_weight[own - margin :]), up_blocks
    )
    grad_rows = group_gather(cot_held, size)
    ahead = lax.ppermute(edge_high, "grp", [(i, i + 1) for i in range(size - 1)])
    behind = lax.ppermute(edge_low, "grp", [(i + 1, i) for i in range(size - 1)])
    output_wide = cut(
        jnp.concatenate([ahead, output_weight, behind]), margin - offset, width, 0
    )
    wide_row = jnp.arange(width, dtype=jnp.int32)[:, None]
    wide_mine = (wide_row >= offset) & (wide_row < offset + own)
    output_mine = put(
        jnp.zeros((width, D), bf16), output_weight, offset, 0
    )

    segment_ids = segments[0]
    relative = lambda whole: jnp.concatenate(
        [cut(whole, (rank ^ o) * count, count, 0) for o in order]
    )
    position = relative(jnp.arange(seq, dtype=jnp.int32))
    segment_rows = relative(segment_ids)
    doc_begin = jnp.sum((segment_ids[:, None] < segment_rows[None, :]).astype(jnp.int32), axis=0)
    bounds = jnp.concatenate([doc_begin[None], position[None], jnp.zeros((6, seq), jnp.int32)])

    normal_a = (norm_rows(rows_all.astype(f32))[0] * vectors[0] + vectors[1]).astype(bf16)
    take = lambda vector: cut(vector, begin * HD, width, 0)
    packed_bias = jnp.concatenate([take(vectors[2]), jnp.zeros((width,), f32), take(vectors[3])])
    projected = (contract(packed_cols, normal_a, 0, 1) + packed_bias[:, None]).astype(bf16)
    mixed, totals = attend(projected, bounds, rank, size, heads)
    attn_part = contract(mixed, output_mine, 0, 0)
    rows_float = rows_own.astype(f32)
    residual = rows_float + group_scatter_sum(attn_part, size) + vectors[4]
    normed_second, inv_second = norm_rows(residual)
    normal_c_own = (normed_second * vectors[5] + vectors[6]).astype(bf16)
    normal_c = group_gather(normal_c_own, size)
    pre_act = contract(normal_c, up_cols, 1, 0) + hidden_bias.astype(f32)
    gelu_value, gelu_slope = gelu_parts(pre_act)
    hidden = gelu_value.astype(bf16)

    grad_hidden = contract(grad_rows, down_weight, 1, 1)
    grad_pre = (grad_hidden * gelu_slope).astype(bf16)
    grad_c_part = contract(grad_pre, up_cols, 1, 1)
    grad_c = group_scatter_sum(grad_c_part, size)
    grad_down = contract(grad_rows, hidden, 0, 0)
    grad_up = contract(normal_c, grad_pre, 0, 0)
    layer_part = contract(hidden, down_weight, 1, 0)

    share = reps // size
    low_bits, all_bits = log2(size), log2(reps)
    down_axis = lambda bit: all_bits - 1 - bit
    down_parts = halve_rows(natural_rows(grad_down, reps), 0, reps, down_axis(0))
    up_order = list(reversed(range(low_bits))) + list(range(low_bits, all_bits))
    up_parts = halve_rows(grad_up, up_order[0], reps, 0)

    grad_float = cotangent[0].astype(f32)
    grad_resid = grad_float + norm_back(grad_c, normed_second, inv_second, vectors[5])
    grad_attn_own = grad_resid.astype(bf16)
    grad_attn = group_gather(grad_attn_own, size)

    grad_mixed = contract(output_wide, grad_attn, 1, 1).astype(bf16)
    mixed_mine = cut(mixed, offset, own, 0)
    grad_output = contract(grad_attn, mixed_mine, 0, 1)
    out_parts = quad_step(grad_output.reshape(share, size, D // reps, own), 1, reps, size)
    down_parts = tie(down_parts, grad_mixed)
    up_parts = tie(up_parts, grad_mixed)
    for step in range(1, all_bits - 1):
        down_piece, up_piece = add_parts(down_parts, bf16), add_parts(up_parts, bf16)
        down_parts = halve_rows(down_piece, step, reps, down_axis(step))
        if step < low_bits:
            up_parts = halve_rows(up_piece, up_order[step], reps, 0)
        else:
            up_parts = halve_lanes(up_piece, up_order[step], reps)
    held = tie(grad_mixed, (down_parts[0], up_parts[0], out_parts[0]))
    grad_packed_rows = attend_back(projected, mixed, held, totals, bounds, rank, size, heads)
    grad_mine = cut(grad_packed_rows, offset, own, 1)
    grad_packed = contract(normal_a, grad_mine.reshape(3 * own, seq), 0, 1)
    packed_parts = quad_step(grad_packed.reshape(size, own, 3 * own), 0, reps, size)

    down_parts, up_parts = tie((down_parts, up_parts), packed_parts[0])
    down_last = halve_rows(add_parts(down_parts, bf16), all_bits - 1, reps, down_axis(all_bits - 1))
    up_last = halve_lanes(add_parts(up_parts, bf16), all_bits - 1, reps)

    grad_masked = jnp.where(wide_mine[None], grad_packed_rows, jnp.zeros_like(grad_packed_rows))
    grad_masked = tie(grad_masked, packed_parts[0])
    grad_a_part = contract(grad_masked.reshape(3 * width, seq), packed_cols, 0, 1)
    grad_a = group_scatter_sum(grad_a_part, size)
    out_parts = tie(out_parts, grad_a)
    out_piece = add_parts(out_parts, bf16)
    for bit in reversed(range(low_bits, all_bits)):
        out_piece = add_parts(halve_rows(out_piece, bit, reps, 0), f32)
    final_output = out_piece.reshape(D // reps, own).T
    layer_rows = residual + group_scatter_sum(layer_part, size) + vectors[7]
    normed_first, inv_first = norm_rows(rows_float)
    grad_in = grad_resid + norm_back(grad_a, normed_first, inv_first, vectors[0])

    def spread(values, length):
        return put(
            jnp.zeros((length,), f32), values, rank * values.shape[0], 0
        )

    sums = jnp.concatenate(
        [
            jnp.sum(grad_a * normed_first, axis=0),
            jnp.sum(grad_a, axis=0),
            spread(jnp.sum(grad_mine[0].astype(f32), axis=1), D),
            spread(jnp.sum(grad_mine[2].astype(f32), axis=1), D),
            jnp.sum(grad_attn_own.astype(f32), axis=0),
            jnp.sum(grad_c * normed_second, axis=0),
            jnp.sum(grad_c, axis=0),
            spread(jnp.sum(grad_pre.astype(f32), axis=0), hidden_all),
            jnp.sum(grad_float, axis=0),
        ]
    )
    sums_begun = sum_over(sums.reshape(-1, 128), "grp", size)

    piece = add_parts(tie(packed_parts, sums_begun), bf16)
    piece = jnp.stack([piece[:, own * t : own * (t + 1)] for t in range(3)])
    for bit in range(low_bits, all_bits):
        halves = halve_lanes(piece, bit, reps)
        piece = add_parts(halves, bf16)
    sums = sum_over(tie(sums_begun, piece), "rep", reps).reshape(-1)
    rounds = match_rounds(reps, 3)
    table = jnp.array(rounds, jnp.int32)
    unit = rank * share + piece_of(rep_rank, reps, size)[0]
    origin = [[0] * 3 for _ in range(reps)]
    received = []
    for turn, chosen in enumerate(rounds):
        route = []
        for r in range(reps):
            row_part, lane_part = piece_of(r, reps, size)
            for g in range(size):
                v = g * share + row_part
                where = reps * chosen[v] + v
                origin[where // 3][where % 3] = turn
                route.append((r * size + g, (where // 3) * size + lane_part))
        sent = pick(piece, table[turn, unit], 0)
        received.append(lax.ppermute(sent, ("rep", "grp"), route))
    down_last, up_last = tie((down_last, up_last), halves[0])
    final_down = add_parts(down_last, f32).reshape(D // reps, hidden_own).T
    route = []
    for r in range(reps):
        row_part, lane_part = piece_of(r, reps, size)
        for g in range(size):
            route.append((r * size + g, (g * share + row_part) * size + lane_part))
    final_up = lax.ppermute(add_parts(up_last, bf16), ("rep", "grp"), route).astype(f32)

    received = jnp.stack(received)
    owner = jnp.array(origin, jnp.int32)[rep_rank]
    final_packed = jnp.concatenate(
        [pick(received, owner[k], 0) for k in range(3)], axis=1
    ).astype(f32)

    ends = [D, 2 * D, 3 * D, 4 * D, 5 * D, 6 * D, 7 * D, 7 * D + hidden_all]
    return (
        layer_rows[None],
        grad_in[None],
        final_packed,
        final_output,
        final_up,
        final_down,
        *jnp.split(sums, ends),
    )


def solution(mesh):
    in_specs = (
        P("rep", "grp", None),
        P("rep", None),
        P("rep", "grp", None),
        P("grp", None),
        P("grp", None),
        P("grp", None),
        P("grp", None),
    ) + (P("grp"),) * 9
    out_specs = (
        P("rep", "grp", None),
        P("rep", "grp", None),
        P("grp", "rep"),
        P("grp", "rep"),
        P("grp", "rep"),
        P("grp", "rep"),
    ) + (P(),) * 9

    def body(*args):
        return shards(mesh.shape["rep"], mesh.shape["grp"], *args)

    return jax.shard_map(body, mesh=mesh, in_specs=in_specs, out_specs=out_specs, check_vma=False)
```

```python
import math

import jax
import jax.numpy as jnp
from jax import lax
from jax.experimental import pallas as pl
from jax.experimental.pallas import tpu as pltpu
from jax.sharding import PartitionSpec as P

D = 1088
HEADS = 17
HD = 64

epsilon = 1e-05
gelu_factor = 0.7978845608028654
masked_score = -1e30
f32 = jnp.float32
bf16 = jnp.bfloat16


def gelu_parts(pre_act):
    inner = gelu_factor * (pre_act + 0.044715 * pre_act * pre_act * pre_act)
    tanh_value = jnp.tanh(inner)
    gelu_value = 0.5 * pre_act * (1.0 + tanh_value)
    gelu_slope = 0.5 * (1.0 + tanh_value) + 0.5 * pre_act * (
        1.0 - tanh_value * tanh_value
    ) * gelu_factor * (1.0 + 3.0 * 0.044715 * pre_act * pre_act)
    return (gelu_value, gelu_slope)


def row_stats(field):
    row_mean = jnp.mean(field, axis=-1, keepdims=True)
    centered = field - row_mean
    inv_std = lax.rsqrt(jnp.mean(centered * centered, axis=-1, keepdims=True) + epsilon)
    return (row_mean, inv_std)


def norm_rows(field):
    row_mean, inv_std = row_stats(field)
    return ((field - row_mean) * inv_std, inv_std)


def norm_back(grad_out, normed, inv_std, gain_row):
    scaled = grad_out * gain_row
    return inv_std * (
        scaled
        - jnp.mean(scaled, axis=-1, keepdims=True)
        - normed * jnp.mean(scaled * normed, axis=-1, keepdims=True)
    )


def contract(left, right, left_dim, right_dim):
    return lax.dot_general(
        left, right, (((left_dim,), (right_dim,)), ((), ())), preferred_element_type=f32
    )


def swap(value, axis, size, bit):
    return lax.ppermute(value, axis, [(i, i ^ bit) for i in range(size)])


def starts_at(value, start, axis):
    starts = [0] * value.ndim
    starts[axis] = start
    return starts


def cut(value, start, length, axis):
    sizes = list(value.shape)
    sizes[axis] = length
    starts = starts_at(value, start, axis)
    return lax.dynamic_slice(value, starts, sizes, allow_negative_indices=False)


def pick(value, index, axis):
    return lax.squeeze(cut(value, index, 1, axis), (axis,))


def put(whole, part, start, axis):
    starts = starts_at(whole, start, axis)
    return lax.dynamic_update_slice(whole, part, starts, allow_negative_indices=False)


def log2(count):
    return count.bit_length() - 1


def relative_order(size):
    order = [0]
    bit = size // 2
    while bit:
        order = order + [o ^ bit for o in order]
        bit //= 2
    return order


def group_gather(value, size):
    bit = size // 2
    while bit:
        value = jnp.concatenate([value, swap(value, "grp", size, bit)])
        bit //= 2
    return value


def group_scatter_sum(value, size):
    bit = 1
    while bit < size:
        half = value.shape[0] // 2
        moved = swap(value[half:].astype(bf16), "grp", size, bit)
        value = value[:half] + moved.astype(f32)
        bit *= 2
    return value


def place_of(j, flip, size):
    return j ^ flip if 2 * j >= size else j


def place_kernel(rank_ref, flip_ref, *refs):
    out_ref = refs[-1]
    for j, ref in enumerate(refs[:-1]):
        rows = ref.shape[0]
        place = rank_ref[0] ^ place_of(j, flip_ref[0], len(refs) - 1)
        out_ref[pl.ds(pl.multiple_of(place * rows, 16), rows), :] = ref[...]


def place_rows(blocks, rank, flip):
    rows, cols = blocks[0].shape
    size = len(blocks)
    if rows % 16:
        whole = jnp.zeros((rows * size, cols), blocks[0].dtype)
        for j, block in enumerate(blocks):
            whole = put(whole, block, (rank ^ place_of(j, flip, size)) * rows, 0)
        return whole
    return pl.pallas_call(
        place_kernel,
        grid_spec=pltpu.PrefetchScalarGridSpec(
            num_scalar_prefetch=2,
            grid=(1,),
            in_specs=[pl.BlockSpec((rows, cols), lambda i, *_: (0, 0))] * size,
            out_specs=pl.BlockSpec((rows * size, cols), lambda i, *_: (0, 0)),
        ),
        out_shape=jax.ShapeDtypeStruct((rows * size, cols), blocks[0].dtype),
        cost_estimate=pl.CostEstimate(
            flops=0, transcendentals=0, bytes_accessed=4 * rows * size * cols
        ),
    )(rank.reshape(1), flip.reshape(1), *blocks)


def first_head(rank, size):
    return lax.div(rank * (D // size), HD)


def pack_kernel(width, rank_ref, source_ref, *out_refs):
    for j, out_ref in enumerate(out_refs):
        begin = first_head(rank_ref[0] ^ j, len(out_refs)) * HD
        parts = []
        for t in range(3):
            shift = D * t % 128
            start = pl.multiple_of(begin + (D * t - shift), 128)
            parts.append(source_ref[:, pl.ds(start, shift + width)][:, shift:])
        out_ref[...] = jnp.concatenate(parts, axis=1)


def pack_columns(weight, begins, width, rank, size):
    starts = [min(b * HD, D - width) for b in begins]
    if any(start % 128 or start != b * HD for start, b in zip(starts, begins)):
        sets = jnp.stack(
            [
                jnp.concatenate([weight[:, D * t + o : D * t + o + width] for t in range(3)], axis=1)
                for o in starts
            ]
        )
        return [pick(sets, rank ^ j, 0) for j in range(size)]
    rows = weight.shape[0]
    return pl.pallas_call(
        lambda *refs: pack_kernel(width, *refs),
        grid_spec=pltpu.PrefetchScalarGridSpec(
            num_scalar_prefetch=1,
            grid=(1,),
            in_specs=[pl.BlockSpec(weight.shape, lambda i, _: (0, 0))],
            out_specs=[pl.BlockSpec((rows, 3 * width), lambda i, _: (0, 0))] * size,
        ),
        out_shape=[jax.ShapeDtypeStruct((rows, 3 * width), weight.dtype)] * size,
        cost_estimate=pl.CostEstimate(
            flops=0, transcendentals=0, bytes_accessed=14 * rows * width * size
        ),
        name="pack_columns",
    )(rank.reshape(1), weight)


def tie(values, deps):
    return lax.optimization_barrier((values, deps))[0]


def sum_over(vector, axis, count):
    bit = 1
    while bit < count:
        moved = swap(vector, axis, count, bit)
        vector = vector + moved
        bit *= 2
    return vector


def rep_bit(bit):
    return (lax.axis_index("rep") >> bit) & 1


def add_parts(parts, dtype):
    total = parts[0].astype(f32)
    for part in parts[1:]:
        total = total + part.astype(f32)
    return total.astype(dtype)


def halve_rows(value, bit, reps, axis):
    mine = rep_bit(bit)
    half = value.shape[axis] // 2
    keep = cut(value, mine * half, half, axis)
    give = cut(value, (1 - mine) * half, half, axis).astype(bf16)
    return keep, swap(give, "rep", reps, 1 << bit)


def halve_lanes(value, bit, reps):
    mine = rep_bit(bit) == 1
    half = value.shape[-1] // 2
    low, high = value[..., :half], value[..., half:]
    give = jnp.where(mine, low, high).astype(bf16)
    return jnp.where(mine, high, low), swap(give, "rep", reps, 1 << bit)


def natural_rows(value, reps):
    return value.reshape((2,) * log2(reps) + (value.shape[0] // reps,) + value.shape[1:])


def quad_step(value, axis, reps, size):
    low = lax.axis_index("rep") & (size - 1)
    block = lambda o: pick(value, low ^ o, axis)
    gives = [block(o).astype(bf16) for o in range(1, size)]
    return [block(0)] + [swap(give, "rep", reps, o + 1) for o, give in enumerate(gives)]


def piece_of(rep, reps, size):
    row_part = 0
    for bit in range(log2(size), log2(reps)):
        row_part = 2 * row_part + ((rep >> bit) & 1)
    return row_part, rep & (size - 1)


def match_rounds(reps, kinds):
    left = {v: set(range(kinds)) for v in range(reps)}
    rounds = []
    for _ in range(kinds):
        owner = {}

        def place(v, seen):
            for kind in sorted(left[v]):
                target = (reps * kind + v) // kinds
                if target in seen:
                    continue
                seen.add(target)
                if target not in owner or place(owner[target][0], seen):
                    owner[target] = (v, kind)
                    return True
            return False

        for v in range(reps):
            place(v, set())
        chosen = [0] * reps
        for v, kind in owner.values():
            chosen[v] = kind
            left[v].discard(kind)
        rounds.append(chosen)
    return rounds


def mask_bias(bias_ref, bounds_ref, rank_ref, blocks):
    order = relative_order(blocks)
    tokens = bias_ref.shape[0] // blocks
    for block in range(blocks):
        for part in range(bias_ref.shape[1] // 128):
            lanes = slice(128 * part, 128 * (part + 1))
            shape = (tokens, 128)
            key_pos = (rank_ref[0] ^ order[block]) * tokens + lax.broadcasted_iota(jnp.int32, shape, 0)
            inside = (key_pos >= bounds_ref[0:1, lanes]) & (key_pos <= bounds_ref[1:2, lanes])
            bias_ref[pl.ds(block * tokens, tokens), lanes] = jnp.where(inside, 0.0, masked_score)


def attend_kernel(blocks, rank_ref, bounds_ref, query_ref, key_ref, value_ref, mixed_ref, total_ref, bias_ref):
    @pl.when(pl.program_id(0) == 0)
    def _():
        mask_bias(bias_ref, bounds_ref, rank_ref, blocks)

    keys = key_ref[...]
    values = value_ref[...]
    for part in range(query_ref.shape[1] // 128):
        lanes = slice(128 * part, 128 * (part + 1))
        queries = query_ref[:, lanes]
        scores = contract(keys, queries, 0, 0) * (1.0 / math.sqrt(HD)) + bias_ref[:, lanes]
        row_max = jnp.max(scores, axis=0, keepdims=True)
        weights = jnp.exp(scores - row_max)
        row_sum = jnp.sum(weights, axis=0, keepdims=True)
        total_ref[0, :, lanes] = row_max + jnp.log(row_sum)
        probs = (weights * (1.0 / row_sum)).astype(bf16)
        mixed_ref[:, lanes] = contract(values, probs, 1, 0).astype(bf16)


def attend_back_kernel(
    blocks,
    rank_ref,
    bounds_ref,
    query_ref,
    key_ref,
    value_ref,
    mixed_ref,
    grad_ref,
    total_ref,
    out_ref,
    bias_ref,
    probs_ref,
    slope_ref,
):
    @pl.when(pl.program_id(0) == 0)
    def _():
        mask_bias(bias_ref, bounds_ref, rank_ref, blocks)

    keys = key_ref[...]
    values = value_ref[...]
    scale = 1.0 / math.sqrt(HD)
    for part in range(query_ref.shape[1] // 128):
        lanes = slice(128 * part, 128 * (part + 1))
        queries = query_ref[:, lanes]
        grads = grad_ref[:, lanes]
        scores = contract(keys, queries, 0, 0) * scale + bias_ref[:, lanes]
        probs = jnp.exp(scores - total_ref[0, :, lanes])
        delta = jnp.sum(grads.astype(f32) * mixed_ref[:, lanes].astype(f32), axis=0, keepdims=True)
        grad_probs = contract(values, grads, 0, 0)
        slope = (probs * (grad_probs - delta) * scale).astype(bf16)
        probs_ref[:, lanes] = probs.astype(bf16)
        slope_ref[:, lanes] = slope
        out_ref[0, :, lanes] = contract(keys, slope, 1, 0).astype(bf16)
    slope = slope_ref[...]
    out_ref[1] = contract(query_ref[...], slope, 1, 1).astype(bf16)
    out_ref[2] = contract(grad_ref[...], probs_ref[...], 1, 1).astype(bf16)


def attend(projected, bounds, rank, blocks, heads):
    seq = projected.shape[1]
    row = lambda shift: pl.BlockSpec((HD, seq), lambda h, _: (h + shift, 0))
    return pl.pallas_call(
        lambda *refs: attend_kernel(blocks, *refs),
        grid_spec=pltpu.PrefetchScalarGridSpec(
            num_scalar_prefetch=1,
            grid=(heads,),
            in_specs=[pl.BlockSpec((8, seq), lambda h, _: (0, 0)), row(0), row(heads), row(2 * heads)],
            out_specs=[row(0), pl.BlockSpec((1, 1, seq), lambda h, _: (h, 0, 0))],
            scratch_shapes=[pltpu.VMEM((seq, seq), f32)],
        ),
        out_shape=[
            jax.ShapeDtypeStruct((heads * HD, seq), bf16),
            jax.ShapeDtypeStruct((heads, 1, seq), f32),
        ],
        cost_estimate=pl.CostEstimate(
            flops=4 * heads * seq * seq * HD,
            transcendentals=heads * seq * seq,
            bytes_accessed=8 * heads * HD * seq,
        ),
        name="attend",
    )(rank.reshape(1), bounds, projected, projected, projected)


def attend_back(projected, mixed, grad_mixed, totals, bounds, rank, blocks, heads):
    seq = projected.shape[1]
    row = lambda shift: pl.BlockSpec((HD, seq), lambda h, _: (h + shift, 0))
    return pl.pallas_call(
        lambda *refs: attend_back_kernel(blocks, *refs),
        grid_spec=pltpu.PrefetchScalarGridSpec(
            num_scalar_prefetch=1,
            grid=(heads,),
            in_specs=[
                pl.BlockSpec((8, seq), lambda h, _: (0, 0)),
                row(0),
                row(heads),
                row(2 * heads),
                row(0),
                row(0),
                pl.BlockSpec((1, 1, seq), lambda h, _: (h, 0, 0)),
            ],
            out_specs=pl.BlockSpec((3, HD, seq), lambda h, _: (0, h, 0)),
            scratch_shapes=[
                pltpu.VMEM((seq, seq), f32),
                pltpu.VMEM((seq, seq), bf16),
                pltpu.VMEM((seq, seq), bf16),
            ],
        ),
        out_shape=jax.ShapeDtypeStruct((3, heads * HD, seq), bf16),
        cost_estimate=pl.CostEstimate(
            flops=10 * heads * seq * seq * HD,
            transcendentals=heads * seq * seq,
            bytes_accessed=16 * heads * HD * seq,
        ),
        name="attend_back",
    )(rank.reshape(1), bounds, projected, projected, projected, mixed, grad_mixed, totals)


def shards(
    reps,
    size,
    tokens,
    segments,
    cotangent,
    packed_weight,
    output_weight,
    up_weight,
    down_weight,
    first_gain,
    first_shift,
    query_bias,
    value_bias,
    output_bias,
    second_gain,
    second_shift,
    hidden_bias,
    down_bias,
):
    rank = lax.axis_index("grp")
    rep_rank = lax.axis_index("rep")
    own = D // size
    hidden_own = hidden_bias.shape[0]
    hidden_all = hidden_own * size
    count = tokens.shape[1]
    seq = segments.shape[1]

    begins = [own * g // HD for g in range(size)]
    heads = max(-(-own * (g + 1) // HD) - begins[g] for g in range(size))
    width = heads * HD
    offsets = [own * g - HD * min(b, HEADS - heads) for g, b in enumerate(begins)]
    margin = max(max(offsets), max(width - own - o for o in offsets))
    begin = first_head(rank, size)
    if begins[-1] * HD > D - width:
        begin = jnp.minimum(begin, HEADS - heads)
    offset = rank * own - HD * begin

    order = relative_order(size)
    rows_own = tokens[0]
    rows_all = group_gather(rows_own, size).astype(f32)
    row_mean, row_inv = row_stats(rows_all)
    packed_give = pack_columns(packed_weight, begins, width, rank, size)
    packed_blocks = [packed_give[0]] + [None] * (size - 1)
    for j in reversed(range(1, size)):
        packed_blocks[j] = swap(packed_give[j], "grp", size, j)
    shorts = (
        first_gain,
        first_shift,
        query_bias,
        value_bias,
        output_bias,
        second_gain,
        second_shift,
        down_bias,
    )
    small = jnp.stack(tie(shorts, packed_give))
    kinds = small.shape[0]
    small = group_gather(small, size).reshape(size, kinds, own)
    vectors = jnp.zeros((size, kinds, own), bf16)
    for i, o in enumerate(order):
        vectors = put(vectors, small[i][None], rank ^ o, 0)
    vectors = vectors.transpose(1, 0, 2).reshape(kinds, D).astype(f32)
    packed_cols = place_rows(packed_blocks, rank, jnp.zeros((), jnp.int32))

    up_sets = jnp.stack([up_weight[:, hidden_own * g : hidden_own * (g + 1)] for g in range(size)])
    flip = rep_rank & 1 if size == 4 else jnp.zeros((), jnp.int32)
    up_blocks = [pick(up_sets, rank, 0)] + [None] * (size - 1)
    if size == 4:
        route = [(r * 4 + g, r * 4 + (g ^ 2 ^ (r & 1))) for r in range(reps) for g in range(4)]
        up_blocks[2] = lax.ppermute(pick(up_sets, rank ^ 2 ^ flip, 0), ("rep", "grp"), route)
        up_blocks[1] = swap(pick(up_sets, rank ^ 1, 0), "grp", size, 1)
        up_blocks[3] = swap(up_blocks[2], "rep", reps, 1)
    else:
        for j in range(1, size):
            up_blocks[j] = swap(pick(up_sets, rank ^ j, 0), "grp", size, j)
    up_cols = place_rows(up_blocks, rank, flip)
    grad_rows = group_gather(cotangent[0], size)
    edge_pairs = [(i, i + 1) for i in range(size - 1)]
    ahead = lax.ppermute(output_weight[own - margin :], "grp", edge_pairs)
    behind = lax.ppermute(output_weight[:margin], "grp", [(j, i) for i, j in edge_pairs])
    output_wide = cut(
        jnp.concatenate([ahead, output_weight, behind]), margin - offset, width, 0
    )
    wide_row = jnp.arange(width, dtype=jnp.int32)[:, None]
    wide_mine = (wide_row >= offset) & (wide_row < offset + own)
    output_mine = put(
        jnp.zeros((width, D), bf16), output_weight, offset, 0
    )

    segment_ids = segments[0]
    relative = lambda whole: jnp.concatenate(
        [cut(whole, (rank ^ o) * count, count, 0) for o in order]
    )
    position = relative(jnp.arange(seq, dtype=jnp.int32))
    segment_rows = relative(segment_ids)
    doc_begin = jnp.sum((segment_ids[:, None] < segment_rows[None, :]).astype(jnp.int32), axis=0)
    bounds = jnp.concatenate([doc_begin[None], position[None], jnp.zeros((6, seq), jnp.int32)])

    normal_a = ((rows_all - row_mean) * row_inv * vectors[0] + vectors[1]).astype(bf16)
    take = lambda vector: cut(vector, begin * HD, width, 0)
    packed_bias = jnp.concatenate([take(vectors[2]), jnp.zeros((width,), f32), take(vectors[3])])
    projected = (contract(packed_cols, normal_a, 0, 1) + packed_bias[:, None]).astype(bf16)
    mixed, totals = attend(projected, bounds, rank, size, heads)
    attn_part = contract(mixed, output_mine, 0, 0)
    rows_float = rows_own.astype(f32)
    residual = rows_float + group_scatter_sum(attn_part, size) + vectors[4]
    normed_second, inv_second = norm_rows(residual)
    normal_c_own = (normed_second * vectors[5] + vectors[6]).astype(bf16)
    normal_c = group_gather(normal_c_own, size)
    pre_act = contract(normal_c, up_cols, 1, 0) + hidden_bias.astype(f32)
    gelu_value, gelu_slope = gelu_parts(pre_act)
    hidden = gelu_value.astype(bf16)

    grad_hidden = contract(grad_rows, down_weight, 1, 1)
    grad_pre = (grad_hidden * gelu_slope).astype(bf16)
    grad_c_part = contract(grad_pre, up_cols, 1, 1)
    grad_c = group_scatter_sum(grad_c_part, size)
    grad_down = contract(grad_rows, hidden, 0, 0)
    grad_up = contract(normal_c, grad_pre, 0, 0)
    layer_part = contract(hidden, down_weight, 1, 0)

    share = reps // size
    low_bits, all_bits = log2(size), log2(reps)
    down_axis = lambda bit: all_bits - 1 - bit
    down_parts = halve_rows(natural_rows(grad_down, reps), 0, reps, down_axis(0))
    up_order = list(reversed(range(low_bits))) + list(range(low_bits, all_bits))
    up_parts = halve_rows(grad_up, up_order[0], reps, 0)

    grad_float = cotangent[0].astype(f32)
    grad_resid = grad_float + norm_back(grad_c, normed_second, inv_second, vectors[5])
    grad_attn_own = grad_resid.astype(bf16)
    grad_attn = group_gather(grad_attn_own, size)

    grad_mixed = contract(output_wide, grad_attn, 1, 1).astype(bf16)
    for step in range(1, all_bits - 1):
        down_parts = halve_rows(add_parts(down_parts, bf16), step, reps, down_axis(step))
    held = grad_mixed
    grad_packed_rows = attend_back(projected, mixed, held, totals, bounds, rank, size, heads)
    grad_mine = cut(grad_packed_rows, offset, own, 1)
    grad_packed = contract(normal_a, grad_mine.reshape(3 * own, seq), 0, 1)
    packed_parts = quad_step(grad_packed.reshape(size, own, 3 * own), 0, reps, size)

    down_last = halve_rows(add_parts(down_parts, bf16), all_bits - 1, reps, down_axis(all_bits - 1))
    for step in range(1, all_bits - 1):
        up_piece = add_parts(up_parts, bf16)
        if step < low_bits:
            up_parts = halve_rows(up_piece, up_order[step], reps, 0)
        else:
            up_parts = halve_lanes(up_piece, up_order[step], reps)

    grad_masked = jnp.where(wide_mine[None], grad_packed_rows, jnp.zeros_like(grad_packed_rows))
    grad_a_part = contract(grad_masked.reshape(3 * width, seq), packed_cols, 0, 1)
    grad_a = group_scatter_sum(grad_a_part, size)
    mixed_mine = cut(mixed, offset, own, 0)
    grad_output = contract(grad_attn, mixed_mine, 0, 1)
    out_parts = quad_step(grad_output.reshape(share, size, D // reps, own), 1, reps, size)
    up_last = halve_lanes(add_parts(up_parts, bf16), all_bits - 1, reps)
    layer_rows = residual + group_scatter_sum(layer_part, size) + vectors[7]
    normed_first, inv_first = norm_rows(rows_float)
    grad_in = grad_resid + norm_back(grad_a, normed_first, inv_first, vectors[0])

    def spread(values, length):
        return put(
            jnp.zeros((length,), f32), values, rank * values.shape[0], 0
        )

    sums = jnp.concatenate(
        [
            jnp.sum(grad_a * normed_first, axis=0),
            jnp.sum(grad_a, axis=0),
            spread(jnp.sum(grad_mine[0].astype(f32), axis=1), D),
            spread(jnp.sum(grad_mine[2].astype(f32), axis=1), D),
            jnp.sum(grad_attn_own.astype(f32), axis=0),
            jnp.sum(grad_c * normed_second, axis=0),
            jnp.sum(grad_c, axis=0),
            spread(jnp.sum(grad_pre.astype(f32), axis=0), hidden_all),
            jnp.sum(grad_float, axis=0),
        ]
    )
    sums = sum_over(sum_over(sums.reshape(-1, 128), "grp", size), "rep", reps)

    packed_parts, sums = lax.optimization_barrier((packed_parts, sums))
    piece = add_parts(packed_parts, bf16)
    piece = jnp.stack([piece[:, own * t : own * (t + 1)] for t in range(3)])
    for bit in range(low_bits, all_bits):
        halves = halve_lanes(piece, bit, reps)
        piece = add_parts(halves, bf16)
    rounds = match_rounds(reps, 3)
    table = jnp.array(rounds, jnp.int32)
    unit = rank * share + piece_of(rep_rank, reps, size)[0]
    origin = [[0] * 3 for _ in range(reps)]
    received = []
    for turn, chosen in enumerate(rounds):
        route = []
        for r in range(reps):
            row_part, lane_part = piece_of(r, reps, size)
            for g in range(size):
                v = g * share + row_part
                where = reps * chosen[v] + v
                origin[where // 3][where % 3] = turn
                route.append((r * size + g, (where // 3) * size + lane_part))
        sent = pick(piece, table[turn, unit], 0)
        received.append(lax.ppermute(sent, ("rep", "grp"), route))
    out_piece = add_parts(out_parts, bf16)
    for bit in reversed(range(low_bits, all_bits)):
        out_piece = add_parts(halve_rows(out_piece, bit, reps, 0), f32)
    final_output = out_piece.reshape(D // reps, own).T
    final_down = add_parts(down_last, f32).reshape(D // reps, hidden_own).T
    route = []
    for r in range(reps):
        row_part, lane_part = piece_of(r, reps, size)
        for g in range(size):
            route.append((r * size + g, (g * share + row_part) * size + lane_part))
    final_up = lax.ppermute(add_parts(up_last, bf16), ("rep", "grp"), route).astype(f32)

    received = jnp.stack(received)
    owner = jnp.array(origin, jnp.int32)[rep_rank]
    final_packed = jnp.concatenate(
        [pick(received, owner[k], 0) for k in range(3)], axis=1
    ).astype(f32)

    ends = [D, 2 * D, 3 * D, 4 * D, 5 * D, 6 * D, 7 * D, 7 * D + hidden_all]
    return (
        layer_rows[None],
        grad_in[None],
        final_packed,
        final_output,
        final_up,
        final_down,
        *jnp.split(sums.reshape(-1), ends),
    )


def solution(mesh):
    in_specs = (
        P("rep", "grp", None),
        P("rep", None),
        P("rep", "grp", None),
        P("grp", None),
        P("grp", None),
        P("grp", None),
        P("grp", None),
    ) + (P("grp"),) * 9
    out_specs = (
        P("rep", "grp", None),
        P("rep", "grp", None),
        P("grp", "rep"),
        P("grp", "rep"),
        P("grp", "rep"),
        P("grp", "rep"),
    ) + (P(),) * 9

    def body(*args):
        return shards(mesh.shape["rep"], mesh.shape["grp"], *args)

    return jax.shard_map(body, mesh=mesh, in_specs=in_specs, out_specs=out_specs, check_vma=False)
```

```python
import math

import jax
import jax.numpy as jnp
from jax import lax
from jax.experimental import pallas as pl
from jax.experimental.pallas import tpu as pltpu
from jax.sharding import PartitionSpec as P

D = 1088
HEADS = 17
HD = 64

GRP, REP = "grp", "rep"
epsilon = 1e-05
gelu_factor = 0.7978845608028654
masked_score = -1e30
f32 = jnp.float32
bf16 = jnp.bfloat16


def gelu_parts(pre_act):
    inner = gelu_factor * (pre_act + 0.044715 * pre_act * pre_act * pre_act)
    tanh_value = jnp.tanh(inner)
    gelu_value = 0.5 * pre_act * (1.0 + tanh_value)
    gelu_slope = 0.5 * (1.0 + tanh_value) + 0.5 * pre_act * (
        1.0 - tanh_value * tanh_value
    ) * gelu_factor * (1.0 + 3.0 * 0.044715 * pre_act * pre_act)
    return (gelu_value, gelu_slope)


def row_stats(field):
    row_mean = jnp.mean(field, axis=-1, keepdims=True)
    centered = field - row_mean
    inv_std = lax.rsqrt(jnp.mean(centered * centered, axis=-1, keepdims=True) + epsilon)
    return (row_mean, inv_std)


def norm_rows(field):
    row_mean, inv_std = row_stats(field)
    return ((field - row_mean) * inv_std, inv_std)


def norm_back(grad_out, normed, inv_std, gain_row):
    scaled = grad_out * gain_row
    return inv_std * (
        scaled
        - jnp.mean(scaled, axis=-1, keepdims=True)
        - normed * jnp.mean(scaled * normed, axis=-1, keepdims=True)
    )


def contract(left, right, left_dim, right_dim):
    return lax.dot_general(
        left, right, (((left_dim,), (right_dim,)), ((), ())), preferred_element_type=f32
    )


def swap(value, axis, size, bit):
    return lax.ppermute(value, axis, [(i, i ^ bit) for i in range(size)])


def starts_at(value, start, axis):
    starts = [0] * value.ndim
    starts[axis] = start
    return starts


def cut(value, start, length, axis):
    sizes = list(value.shape)
    sizes[axis] = length
    starts = starts_at(value, start, axis)
    return lax.dynamic_slice(value, starts, sizes, allow_negative_indices=False)


def pick(value, index, axis):
    return lax.squeeze(cut(value, index, 1, axis), (axis,))


def put(whole, part, start, axis):
    starts = starts_at(whole, start, axis)
    return lax.dynamic_update_slice(whole, part, starts, allow_negative_indices=False)


def log2(count):
    return count.bit_length() - 1


def relative_order(size):
    order = [0]
    bit = size // 2
    while bit:
        order = order + [o ^ bit for o in order]
        bit //= 2
    return order


def group_gather(value, size):
    bit = size // 2
    while bit:
        value = jnp.concatenate([value, swap(value, GRP, size, bit)])
        bit //= 2
    return value


def group_scatter_sum(value, size):
    bit = 1
    while bit < size:
        half = value.shape[0] // 2
        moved = swap(value[half:].astype(bf16), GRP, size, bit)
        value = value[:half] + moved.astype(f32)
        bit *= 2
    return value


def place_of(j, flip, size):
    return j ^ flip if 2 * j >= size else j


def place_kernel(rank_ref, flip_ref, *refs):
    out_ref = refs[-1]
    for j, ref in enumerate(refs[:-1]):
        rows = ref.shape[0]
        place = rank_ref[0] ^ place_of(j, flip_ref[0], len(refs) - 1)
        out_ref[pl.ds(pl.multiple_of(place * rows, 16), rows), :] = ref[...]


def place_rows(blocks, rank, flip):
    rows, cols = blocks[0].shape
    size = len(blocks)
    if rows % 16:
        whole = jnp.zeros((rows * size, cols), blocks[0].dtype)
        for j, block in enumerate(blocks):
            whole = put(whole, block, (rank ^ place_of(j, flip, size)) * rows, 0)
        return whole
    return pl.pallas_call(
        place_kernel,
        grid_spec=pltpu.PrefetchScalarGridSpec(
            num_scalar_prefetch=2,
            grid=(1,),
            in_specs=[pl.BlockSpec((rows, cols), lambda i, *_: (0, 0))] * size,
            out_specs=pl.BlockSpec((rows * size, cols), lambda i, *_: (0, 0)),
        ),
        out_shape=jax.ShapeDtypeStruct((rows * size, cols), blocks[0].dtype),
        cost_estimate=pl.CostEstimate(
            flops=0, transcendentals=0, bytes_accessed=4 * rows * size * cols
        ),
    )(rank.reshape(1), flip.reshape(1), *blocks)


def first_head(rank, size):
    return lax.div(rank * (D // size), HD)


def pack_kernel(width, rank_ref, source_ref, *out_refs):
    for j, out_ref in enumerate(out_refs):
        begin = first_head(rank_ref[0] ^ j, len(out_refs)) * HD
        parts = []
        for t in range(3):
            shift = D * t % 128
            start = pl.multiple_of(begin + (D * t - shift), 128)
            parts.append(source_ref[:, pl.ds(start, shift + width)][:, shift:])
        out_ref[...] = jnp.concatenate(parts, axis=1)


def pack_columns(weight, begins, width, rank, size):
    starts = [min(b * HD, D - width) for b in begins]
    if any(start % 128 or start != b * HD for start, b in zip(starts, begins)):
        sets = jnp.stack(
            [
                jnp.concatenate([weight[:, D * t + o : D * t + o + width] for t in range(3)], axis=1)
                for o in starts
            ]
        )
        return [pick(sets, rank ^ j, 0) for j in range(size)]
    rows = weight.shape[0]
    return pl.pallas_call(
        lambda *refs: pack_kernel(width, *refs),
        grid_spec=pltpu.PrefetchScalarGridSpec(
            num_scalar_prefetch=1,
            grid=(1,),
            in_specs=[pl.BlockSpec(weight.shape, lambda i, _: (0, 0))],
            out_specs=[pl.BlockSpec((rows, 3 * width), lambda i, _: (0, 0))] * size,
        ),
        out_shape=[jax.ShapeDtypeStruct((rows, 3 * width), weight.dtype)] * size,
        cost_estimate=pl.CostEstimate(
            flops=0, transcendentals=0, bytes_accessed=14 * rows * width * size
        ),
        name="pack",
    )(rank.reshape(1), weight)


def tie(values, deps):
    return lax.optimization_barrier((values, deps))[0]


def sum_over(vector, axis, count):
    bit = 1
    while bit < count:
        moved = swap(vector, axis, count, bit)
        vector = vector + moved
        bit *= 2
    return vector


def rep_bit(bit):
    return (lax.axis_index(REP) >> bit) & 1


def add_parts(parts, dtype):
    total = parts[0].astype(f32)
    for part in parts[1:]:
        total = total + part.astype(f32)
    return total.astype(dtype)


def halve_rows(value, bit, reps, axis):
    mine = rep_bit(bit)
    half = value.shape[axis] // 2
    keep = cut(value, mine * half, half, axis)
    give = cut(value, (1 - mine) * half, half, axis).astype(bf16)
    return keep, swap(give, REP, reps, 1 << bit)


def halve_lanes(value, bit, reps):
    mine = rep_bit(bit) == 1
    half = value.shape[-1] // 2
    low, high = value[..., :half], value[..., half:]
    give = jnp.where(mine, low, high).astype(bf16)
    return jnp.where(mine, high, low), swap(give, REP, reps, 1 << bit)


def natural_rows(value, reps):
    return value.reshape((2,) * log2(reps) + (value.shape[0] // reps,) + value.shape[1:])


def piece_of(rep, reps, size):
    row_part = 0
    for bit in range(log2(size), log2(reps)):
        row_part = 2 * row_part + ((rep >> bit) & 1)
    return row_part, rep & (size - 1)


def match_rounds(reps, kinds):
    left = {v: set(range(kinds)) for v in range(reps)}
    rounds = []
    for _ in range(kinds):
        owner = {}

        def place(v, seen):
            for kind in sorted(left[v]):
                target = (reps * kind + v) // kinds
                if target in seen:
                    continue
                seen.add(target)
                if target not in owner or place(owner[target][0], seen):
                    owner[target] = (v, kind)
                    return True
            return False

        for v in range(reps):
            place(v, set())
        chosen = [0] * reps
        for v, kind in owner.values():
            chosen[v] = kind
            left[v].discard(kind)
        rounds.append(chosen)
    return rounds


def mask_bias(bias_ref, bounds_ref, rank_ref, blocks):
    order = relative_order(blocks)
    tokens = bias_ref.shape[0] // blocks
    for block in range(blocks):
        for part in range(bias_ref.shape[1] // 128):
            lanes = slice(128 * part, 128 * (part + 1))
            shape = (tokens, 128)
            key_pos = (rank_ref[0] ^ order[block]) * tokens + lax.broadcasted_iota(jnp.int32, shape, 0)
            inside = (key_pos >= bounds_ref[0:1, lanes]) & (key_pos <= bounds_ref[1:2, lanes])
            bias_ref[pl.ds(block * tokens, tokens), lanes] = jnp.where(inside, 0.0, masked_score)


def attend_kernel(blocks, rank_ref, bounds_ref, query_ref, key_ref, value_ref, mixed_ref, total_ref, bias_ref):
    @pl.when(pl.program_id(0) == 0)
    def _():
        mask_bias(bias_ref, bounds_ref, rank_ref, blocks)

    keys = key_ref[...]
    values = value_ref[...]
    for part in range(query_ref.shape[1] // 128):
        lanes = slice(128 * part, 128 * (part + 1))
        queries = query_ref[:, lanes]
        scores = contract(keys, queries, 0, 0) * (1.0 / math.sqrt(HD)) + bias_ref[:, lanes]
        row_max = jnp.max(scores, axis=0, keepdims=True)
        weights = jnp.exp(scores - row_max)
        row_sum = jnp.sum(weights, axis=0, keepdims=True)
        total_ref[0, :, lanes] = row_max + jnp.log(row_sum)
        probs = (weights * (1.0 / row_sum)).astype(bf16)
        mixed_ref[:, lanes] = contract(values, probs, 1, 0).astype(bf16)


def attend_back_kernel(
    blocks,
    rank_ref,
    bounds_ref,
    query_ref,
    key_ref,
    value_ref,
    mixed_ref,
    grad_ref,
    total_ref,
    out_ref,
    bias_ref,
    probs_ref,
    slope_ref,
):
    @pl.when(pl.program_id(0) == 0)
    def _():
        mask_bias(bias_ref, bounds_ref, rank_ref, blocks)

    keys = key_ref[...]
    values = value_ref[...]
    scale = 1.0 / math.sqrt(HD)
    for part in range(query_ref.shape[1] // 128):
        lanes = slice(128 * part, 128 * (part + 1))
        queries = query_ref[:, lanes]
        grads = grad_ref[:, lanes]
        scores = contract(keys, queries, 0, 0) * scale + bias_ref[:, lanes]
        probs = jnp.exp(scores - total_ref[0, :, lanes])
        delta = jnp.sum(grads.astype(f32) * mixed_ref[:, lanes].astype(f32), axis=0, keepdims=True)
        grad_probs = contract(values, grads, 0, 0)
        slope = (probs * (grad_probs - delta) * scale).astype(bf16)
        probs_ref[:, lanes] = probs.astype(bf16)
        slope_ref[:, lanes] = slope
        out_ref[0, :, lanes] = contract(keys, slope, 1, 0).astype(bf16)
    slope = slope_ref[...]
    out_ref[1] = contract(query_ref[...], slope, 1, 1).astype(bf16)
    out_ref[2] = contract(grad_ref[...], probs_ref[...], 1, 1).astype(bf16)


def attend(projected, bounds, rank, blocks, heads):
    seq = projected.shape[1]
    row = lambda shift: pl.BlockSpec((HD, seq), lambda h, _: (h + shift, 0))
    return pl.pallas_call(
        lambda *refs: attend_kernel(blocks, *refs),
        grid_spec=pltpu.PrefetchScalarGridSpec(
            num_scalar_prefetch=1,
            grid=(heads,),
            in_specs=[pl.BlockSpec((8, seq), lambda h, _: (0, 0)), row(0), row(heads), row(2 * heads)],
            out_specs=[row(0), pl.BlockSpec((1, 1, seq), lambda h, _: (h, 0, 0))],
            scratch_shapes=[pltpu.VMEM((seq, seq), f32)],
        ),
        out_shape=[
            jax.ShapeDtypeStruct((heads * HD, seq), bf16),
            jax.ShapeDtypeStruct((heads, 1, seq), f32),
        ],
        cost_estimate=pl.CostEstimate(
            flops=4 * heads * seq * seq * HD,
            transcendentals=heads * seq * seq,
            bytes_accessed=8 * heads * HD * seq,
        ),
        name="attend",
    )(rank.reshape(1), bounds, projected, projected, projected)


def attend_back(projected, mixed, grad_mixed, totals, bounds, rank, blocks, heads):
    seq = projected.shape[1]
    row = lambda shift: pl.BlockSpec((HD, seq), lambda h, _: (h + shift, 0))
    return pl.pallas_call(
        lambda *refs: attend_back_kernel(blocks, *refs),
        grid_spec=pltpu.PrefetchScalarGridSpec(
            num_scalar_prefetch=1,
            grid=(heads,),
            in_specs=[
                pl.BlockSpec((8, seq), lambda h, _: (0, 0)),
                row(0),
                row(heads),
                row(2 * heads),
                row(0),
                row(0),
                pl.BlockSpec((1, 1, seq), lambda h, _: (h, 0, 0)),
            ],
            out_specs=pl.BlockSpec((3, HD, seq), lambda h, _: (0, h, 0)),
            scratch_shapes=[
                pltpu.VMEM((seq, seq), f32),
                pltpu.VMEM((seq, seq), bf16),
                pltpu.VMEM((seq, seq), bf16),
            ],
        ),
        out_shape=jax.ShapeDtypeStruct((3, heads * HD, seq), bf16),
        cost_estimate=pl.CostEstimate(
            flops=10 * heads * seq * seq * HD,
            transcendentals=heads * seq * seq,
            bytes_accessed=16 * heads * HD * seq,
        ),
        name="back",
    )(rank.reshape(1), bounds, projected, projected, projected, mixed, grad_mixed, totals)


def shards(
    reps,
    size,
    tokens,
    segments,
    cotangent,
    packed_weight,
    output_weight,
    up_weight,
    down_weight,
    first_gain,
    first_shift,
    query_bias,
    value_bias,
    output_bias,
    second_gain,
    second_shift,
    hidden_bias,
    down_bias,
):
    rank = lax.axis_index(GRP)
    rep_rank = lax.axis_index(REP)
    own = D // size
    hidden_own = hidden_bias.shape[0]
    hidden_all = hidden_own * size
    count = tokens.shape[1]
    seq = segments.shape[1]

    begins = [own * g // HD for g in range(size)]
    heads = max(-(-own * (g + 1) // HD) - begins[g] for g in range(size))
    width = heads * HD
    offsets = [own * g - HD * min(b, HEADS - heads) for g, b in enumerate(begins)]
    margin = max(max(offsets), max(width - own - o for o in offsets))
    begin = first_head(rank, size)
    if begins[-1] * HD > D - width:
        begin = jnp.minimum(begin, HEADS - heads)
    offset = rank * own - HD * begin

    order = relative_order(size)
    rows_own = tokens[0]
    rows_all = group_gather(rows_own, size).astype(f32)
    row_mean, row_inv = row_stats(rows_all)
    packed_give = pack_columns(packed_weight, begins, width, rank, size)
    packed_blocks = [packed_give[0]] + [None] * (size - 1)
    for j in reversed(range(1, size)):
        packed_blocks[j] = swap(packed_give[j], GRP, size, j)
    shorts = (
        first_gain,
        first_shift,
        query_bias,
        value_bias,
        output_bias,
        second_gain,
        second_shift,
        down_bias,
    )
    small = jnp.stack(tie(shorts, packed_give))
    kinds = small.shape[0]
    small = group_gather(small, size).reshape(size, kinds, own)
    vectors = jnp.zeros((size, kinds, own), bf16)
    for i, o in enumerate(order):
        vectors = put(vectors, small[i][None], rank ^ o, 0)
    vectors = vectors.transpose(1, 0, 2).reshape(kinds, D).astype(f32)
    packed_cols = place_rows(packed_blocks, rank, jnp.zeros((), jnp.int32))

    up_sets = jnp.stack([up_weight[:, hidden_own * g : hidden_own * (g + 1)] for g in range(size)])
    flip = rep_rank & 1 if size == 4 else jnp.zeros((), jnp.int32)
    up_blocks = [pick(up_sets, rank, 0)] + [None] * (size - 1)
    if size == 4:
        route = [(r * 4 + g, r * 4 + (g ^ 2 ^ (r & 1))) for r in range(reps) for g in range(4)]
        up_blocks[2] = lax.ppermute(pick(up_sets, rank ^ 2 ^ flip, 0), (REP, GRP), route)
        up_blocks[1] = swap(pick(up_sets, rank ^ 1, 0), GRP, size, 1)
        up_blocks[3] = swap(up_blocks[2], REP, reps, 1)
    else:
        for j in range(1, size):
            up_blocks[j] = swap(pick(up_sets, rank ^ j, 0), GRP, size, j)
    up_cols = place_rows(up_blocks, rank, flip)
    grad_rows = group_gather(cotangent[0], size)
    edge_pairs = [(i, i + 1) for i in range(size - 1)]
    ahead = lax.ppermute(output_weight[own - margin :], GRP, edge_pairs)
    behind = lax.ppermute(output_weight[:margin], GRP, [(j, i) for i, j in edge_pairs])
    output_wide = cut(
        jnp.concatenate([ahead, output_weight, behind]), margin - offset, width, 0
    )
    wide_row = jnp.arange(width, dtype=jnp.int32)[:, None]
    wide_mine = (wide_row >= offset) & (wide_row < offset + own)
    output_mine = put(
        jnp.zeros((width, D), bf16), output_weight, offset, 0
    )

    segment_ids = segments[0]
    relative = lambda whole: jnp.concatenate(
        [cut(whole, (rank ^ o) * count, count, 0) for o in order]
    )
    position = relative(jnp.arange(seq, dtype=jnp.int32))
    segment_rows = relative(segment_ids)
    doc_begin = jnp.sum((segment_ids[:, None] < segment_rows[None, :]).astype(jnp.int32), axis=0)
    bounds = jnp.concatenate([doc_begin[None], position[None], jnp.zeros((6, seq), jnp.int32)])

    normal_a = ((rows_all - row_mean) * row_inv * vectors[0] + vectors[1]).astype(bf16)
    take = lambda vector: cut(vector, begin * HD, width, 0)
    packed_bias = jnp.concatenate([take(vectors[2]), jnp.zeros((width,), f32), take(vectors[3])])
    projected = (contract(packed_cols, normal_a, 0, 1) + packed_bias[:, None]).astype(bf16)
    mixed, totals = attend(projected, bounds, rank, size, heads)
    attn_part = contract(mixed, output_mine, 0, 0)
    rows_float = rows_own.astype(f32)
    residual = rows_float + group_scatter_sum(attn_part, size) + vectors[4]
    normed_second, inv_second = norm_rows(residual)
    normal_c_own = (normed_second * vectors[5] + vectors[6]).astype(bf16)
    normal_c = group_gather(normal_c_own, size)
    pre_act = contract(normal_c, up_cols, 1, 0) + hidden_bias.astype(f32)
    gelu_value, gelu_slope = gelu_parts(pre_act)
    hidden = gelu_value.astype(bf16)

    grad_hidden = contract(grad_rows, down_weight, 1, 1)
    grad_pre = (grad_hidden * gelu_slope).astype(bf16)
    grad_c_part = contract(grad_pre, up_cols, 1, 1)
    grad_c = group_scatter_sum(grad_c_part, size)
    grad_down = contract(grad_rows, hidden, 0, 0)
    grad_up = contract(normal_c, grad_pre, 0, 0)
    layer_part = contract(hidden, down_weight, 1, 0)

    share = reps // size
    low_bits, all_bits = log2(size), log2(reps)
    down_axis = lambda bit: all_bits - 1 - bit
    row_axis = lambda bit: low_bits - 1 - bit

    def step_natural(parts, bit, dtype=bf16):
        return halve_rows(add_parts(parts, dtype), bit, reps, down_axis(bit))

    def step_piece(value, bit):
        if bit < low_bits:
            return halve_rows(value, bit, reps, row_axis(bit))
        return halve_lanes(value, bit, reps)

    down_parts = halve_rows(natural_rows(grad_down, reps), 0, reps, down_axis(0))
    up_parts = step_piece(grad_up.reshape((2,) * low_bits + (own, hidden_own)), 0)

    grad_float = cotangent[0].astype(f32)
    grad_resid = grad_float + norm_back(grad_c, normed_second, inv_second, vectors[5])
    grad_attn_own = grad_resid.astype(bf16)
    grad_attn = group_gather(grad_attn_own, size)

    grad_mixed = contract(output_wide, grad_attn, 1, 1).astype(bf16)
    for step in range(1, all_bits - 1):
        down_parts = step_natural(down_parts, step)
    grad_packed_rows = attend_back(projected, mixed, grad_mixed, totals, bounds, rank, size, heads)
    grad_mine = cut(grad_packed_rows, offset, own, 1)
    grad_packed = contract(normal_a, grad_mine.reshape(3 * own, seq), 0, 1)
    packed_parts = step_piece(grad_packed.reshape((2,) * low_bits + (own, 3 * own)), 0)

    down_last = step_natural(down_parts, all_bits - 1)
    for step in range(1, all_bits):
        up_parts = step_piece(add_parts(up_parts, bf16), step)

    grad_masked = jnp.where(wide_mine[None], grad_packed_rows, jnp.zeros_like(grad_packed_rows))
    grad_a_part = contract(grad_masked.reshape(3 * width, seq), packed_cols, 0, 1)
    grad_a = group_scatter_sum(grad_a_part, size)
    mixed_mine = cut(mixed, offset, own, 0)
    grad_output = contract(grad_attn, mixed_mine, 0, 1)
    out_parts = halve_rows(natural_rows(grad_output, reps), 0, reps, down_axis(0))
    for bit in range(1, all_bits):
        out_parts = step_natural(out_parts, bit)
    final_output = add_parts(out_parts, f32).reshape(D // reps, own).T
    layer_rows = residual + group_scatter_sum(layer_part, size) + vectors[7]
    normed_first, inv_first = norm_rows(rows_float)
    grad_in = grad_resid + norm_back(grad_a, normed_first, inv_first, vectors[0])

    def spread(values, length):
        return put(
            jnp.zeros((length,), f32), values, rank * values.shape[0], 0
        )

    sums = jnp.concatenate(
        [
            jnp.sum(grad_a * normed_first, axis=0),
            jnp.sum(grad_a, axis=0),
            spread(jnp.sum(grad_mine[0].astype(f32), axis=1), D),
            spread(jnp.sum(grad_mine[2].astype(f32), axis=1), D),
            jnp.sum(grad_attn_own.astype(f32), axis=0),
            jnp.sum(grad_c * normed_second, axis=0),
            jnp.sum(grad_c, axis=0),
            spread(jnp.sum(grad_pre.astype(f32), axis=0), hidden_all),
            jnp.sum(grad_float, axis=0),
        ]
    )
    sums = sum_over(sum_over(sums.reshape(-1, 128), GRP, size), REP, reps)

    for bit in range(1, low_bits):
        packed_parts = step_piece(add_parts(packed_parts, bf16), bit)
    piece = add_parts(packed_parts, bf16).reshape(own, 3 * own)
    piece = jnp.stack([piece[:, own * t : own * (t + 1)] for t in range(3)])
    for bit in range(low_bits, all_bits):
        piece = add_parts(halve_lanes(piece, bit, reps), bf16)
    rounds = match_rounds(reps, 3)
    table = jnp.array(rounds, jnp.int32)
    unit = rank * share + piece_of(rep_rank, reps, size)[0]
    origin = [[0] * 3 for _ in range(reps)]
    received = []
    for turn, chosen in enumerate(rounds):
        route = []
        for r in range(reps):
            row_part, lane_part = piece_of(r, reps, size)
            for g in range(size):
                v = g * share + row_part
                where = reps * chosen[v] + v
                origin[where // 3][where % 3] = turn
                route.append((r * size + g, (where // 3) * size + lane_part))
        sent = pick(piece, table[turn, unit], 0)
        received.append(lax.ppermute(sent, (REP, GRP), route))
    final_down = add_parts(down_last, f32).reshape(D // reps, hidden_own).T
    route = []
    for r in range(reps):
        row_part, lane_part = piece_of(r, reps, size)
        for g in range(size):
            route.append((r * size + g, (g * share + row_part) * size + lane_part))
    final_up = lax.ppermute(add_parts(up_parts, bf16).reshape(own, hidden_own // share), (REP, GRP), route).astype(f32)

    received = jnp.stack(received)
    owner = jnp.array(origin, jnp.int32)[rep_rank]
    final_packed = jnp.concatenate(
        [pick(received, owner[k], 0) for k in range(3)], axis=1
    ).astype(f32)

    ends = [D, 2 * D, 3 * D, 4 * D, 5 * D, 6 * D, 7 * D, 7 * D + hidden_all]
    return (
        layer_rows[None],
        grad_in[None],
        final_packed,
        final_output,
        final_up,
        final_down,
        *jnp.split(sums.reshape(-1), ends),
    )


def solution(mesh):
    in_specs = (
        P(REP, GRP, None),
        P(REP, None),
        P(REP, GRP, None),
        P(GRP, None),
        P(GRP, None),
        P(GRP, None),
        P(GRP, None),
    ) + (P(GRP),) * 9
    out_specs = (
        P(REP, GRP, None),
        P(REP, GRP, None),
        P(GRP, REP),
        P(GRP, REP),
        P(GRP, REP),
        P(GRP, REP),
    ) + (P(),) * 9

    def body(*args):
        return shards(mesh.shape[REP], mesh.shape[GRP], *args)

    return jax.shard_map(body, mesh=mesh, in_specs=in_specs, out_specs=out_specs, check_vma=False)
```

```python
import math

import jax
import jax.numpy as jnp
from jax import lax
from jax.experimental import pallas as pl
from jax.experimental.pallas import tpu as pltpu
from jax.sharding import PartitionSpec as P

D = 1088
HEADS = 17
HD = 64

GRP, REP = "grp", "rep"
epsilon = 1e-05
gelu_factor = 0.7978845608028654
masked_score = -1e30
f32 = jnp.float32
bf16 = jnp.bfloat16


def gelu_parts(pre_act):
    inner = gelu_factor * (pre_act + 0.044715 * pre_act * pre_act * pre_act)
    tanh_value = jnp.tanh(inner)
    gelu_value = 0.5 * pre_act * (1.0 + tanh_value)
    gelu_slope = 0.5 * (1.0 + tanh_value) + 0.5 * pre_act * (
        1.0 - tanh_value * tanh_value
    ) * gelu_factor * (1.0 + 3.0 * 0.044715 * pre_act * pre_act)
    return (gelu_value, gelu_slope)


def row_stats(field):
    row_mean = jnp.mean(field, axis=-1, keepdims=True)
    centered = field - row_mean
    inv_std = lax.rsqrt(jnp.mean(centered * centered, axis=-1, keepdims=True) + epsilon)
    return (row_mean, inv_std)


def norm_rows(field):
    row_mean, inv_std = row_stats(field)
    return ((field - row_mean) * inv_std, inv_std)


def norm_back(grad_out, normed, inv_std, gain_row):
    scaled = grad_out * gain_row
    return inv_std * (
        scaled
        - jnp.mean(scaled, axis=-1, keepdims=True)
        - normed * jnp.mean(scaled * normed, axis=-1, keepdims=True)
    )


def contract(left, right, left_dim, right_dim):
    return lax.dot_general(
        left, right, (((left_dim,), (right_dim,)), ((), ())), preferred_element_type=f32
    )


def swap(value, axis, size, bit):
    return lax.ppermute(value, axis, [(i, i ^ bit) for i in range(size)])


def starts_at(value, start, axis):
    starts = [0] * value.ndim
    starts[axis] = start
    return starts


def cut(value, start, length, axis):
    sizes = list(value.shape)
    sizes[axis] = length
    starts = starts_at(value, start, axis)
    return lax.dynamic_slice(value, starts, sizes, allow_negative_indices=False)


def pick(value, index, axis):
    return lax.squeeze(cut(value, index, 1, axis), (axis,))


def put(whole, part, start, axis):
    starts = starts_at(whole, start, axis)
    return lax.dynamic_update_slice(whole, part, starts, allow_negative_indices=False)


def log2(count):
    return count.bit_length() - 1


def relative_order(size):
    order = [0]
    bit = size // 2
    while bit:
        order = order + [o ^ bit for o in order]
        bit //= 2
    return order


def group_gather(value, size):
    bit = size // 2
    while bit:
        value = jnp.concatenate([value, swap(value, GRP, size, bit)])
        bit //= 2
    return value


def group_scatter_sum(value, size):
    bit = 1
    while bit < size:
        half = value.shape[0] // 2
        moved = swap(value[half:].astype(bf16), GRP, size, bit)
        value = value[:half] + moved.astype(f32)
        bit *= 2
    return value


def place_of(j, flip, size):
    return j ^ flip if 2 * j >= size else j


def place_kernel(rank_ref, flip_ref, *refs):
    out_ref = refs[-1]
    for j, ref in enumerate(refs[:-1]):
        rows = ref.shape[0]
        place = rank_ref[0] ^ place_of(j, flip_ref[0], len(refs) - 1)
        out_ref[pl.ds(pl.multiple_of(place * rows, 16), rows), :] = ref[...]


def place_rows(blocks, rank, flip):
    rows, cols = blocks[0].shape
    size = len(blocks)
    if rows % 16:
        whole = jnp.zeros((rows * size, cols), blocks[0].dtype)
        for j, block in enumerate(blocks):
            whole = put(whole, block, (rank ^ place_of(j, flip, size)) * rows, 0)
        return whole
    return pl.pallas_call(
        place_kernel,
        grid_spec=pltpu.PrefetchScalarGridSpec(
            num_scalar_prefetch=2,
            grid=(1,),
            in_specs=[pl.BlockSpec((rows, cols), lambda i, *_: (0, 0))] * size,
            out_specs=pl.BlockSpec((rows * size, cols), lambda i, *_: (0, 0)),
        ),
        out_shape=jax.ShapeDtypeStruct((rows * size, cols), blocks[0].dtype),
        cost_estimate=pl.CostEstimate(
            flops=0, transcendentals=0, bytes_accessed=4 * rows * size * cols
        ),
    )(rank.reshape(1), flip.reshape(1), *blocks)


def first_head(rank, size):
    return lax.div(rank * (D // size), HD)


def pack_kernel(width, rank_ref, source_ref, *out_refs):
    for j, out_ref in enumerate(out_refs):
        begin = first_head(rank_ref[0] ^ j, len(out_refs)) * HD
        parts = []
        for t in range(3):
            shift = D * t % 128
            start = pl.multiple_of(begin + (D * t - shift), 128)
            parts.append(source_ref[:, pl.ds(start, shift + width)][:, shift:])
        out_ref[...] = jnp.concatenate(parts, axis=1)


def pack_columns(weight, begins, width, rank, size):
    starts = [min(b * HD, D - width) for b in begins]
    if any(start % 128 or start != b * HD for start, b in zip(starts, begins)):
        sets = jnp.stack(
            [
                jnp.concatenate([weight[:, D * t + o : D * t + o + width] for t in range(3)], axis=1)
                for o in starts
            ]
        )
        return [pick(sets, rank ^ j, 0) for j in range(size)]
    rows = weight.shape[0]
    return pl.pallas_call(
        lambda *refs: pack_kernel(width, *refs),
        grid_spec=pltpu.PrefetchScalarGridSpec(
            num_scalar_prefetch=1,
            grid=(1,),
            in_specs=[pl.BlockSpec(weight.shape, lambda i, _: (0, 0))],
            out_specs=[pl.BlockSpec((rows, 3 * width), lambda i, _: (0, 0))] * size,
        ),
        out_shape=[jax.ShapeDtypeStruct((rows, 3 * width), weight.dtype)] * size,
        cost_estimate=pl.CostEstimate(
            flops=0, transcendentals=0, bytes_accessed=14 * rows * width * size
        ),
        name="pack",
    )(rank.reshape(1), weight)


def tie(values, deps):
    return lax.optimization_barrier((values, deps))[0]


def sum_over(vector, axis, count):
    bit = 1
    while bit < count:
        moved = swap(vector, axis, count, bit)
        vector = vector + moved
        bit *= 2
    return vector


def rep_bit(bit):
    return (lax.axis_index(REP) >> bit) & 1


def add_parts(parts, dtype):
    total = parts[0].astype(f32)
    for part in parts[1:]:
        total = total + part.astype(f32)
    return total.astype(dtype)


def halve_rows(value, bit, reps, axis):
    mine = rep_bit(bit)
    half = value.shape[axis] // 2
    keep = cut(value, mine * half, half, axis)
    give = cut(value, (1 - mine) * half, half, axis).astype(bf16)
    return keep, swap(give, REP, reps, 1 << bit)


def halve_lanes(value, bit, reps):
    mine = rep_bit(bit) == 1
    half = value.shape[-1] // 2
    low, high = value[..., :half], value[..., half:]
    give = jnp.where(mine, low, high).astype(bf16)
    return jnp.where(mine, high, low), swap(give, REP, reps, 1 << bit)


def natural_rows(value, reps):
    return value.reshape((2,) * log2(reps) + (value.shape[0] // reps,) + value.shape[1:])


def piece_of(rep, reps, size):
    row_part, lane_part = 0, 0
    for bit in range(log2(reps)):
        taken = (rep >> bit) & 1
        if bit < log2(reps // size):
            row_part = 2 * row_part + taken
        else:
            lane_part = 2 * lane_part + taken
    return row_part, lane_part


def match_rounds(reps, kinds):
    left = {v: set(range(kinds)) for v in range(reps)}
    rounds = []
    for _ in range(kinds):
        owner = {}

        def place(v, seen):
            for kind in sorted(left[v]):
                target = (reps * kind + v) // kinds
                if target in seen:
                    continue
                seen.add(target)
                if target not in owner or place(owner[target][0], seen):
                    owner[target] = (v, kind)
                    return True
            return False

        for v in range(reps):
            place(v, set())
        chosen = [0] * reps
        for v, kind in owner.values():
            chosen[v] = kind
            left[v].discard(kind)
        rounds.append(chosen)
    return rounds


def mask_bias(bias_ref, bounds_ref, rank_ref, blocks):
    order = relative_order(blocks)
    tokens = bias_ref.shape[0] // blocks
    for block in range(blocks):
        for part in range(bias_ref.shape[1] // 128):
            lanes = slice(128 * part, 128 * (part + 1))
            shape = (tokens, 128)
            key_pos = (rank_ref[0] ^ order[block]) * tokens + lax.broadcasted_iota(jnp.int32, shape, 0)
            inside = (key_pos >= bounds_ref[0:1, lanes]) & (key_pos <= bounds_ref[1:2, lanes])
            bias_ref[pl.ds(block * tokens, tokens), lanes] = jnp.where(inside, 0.0, masked_score)


def attend_kernel(blocks, rank_ref, bounds_ref, query_ref, key_ref, value_ref, mixed_ref, total_ref, bias_ref):
    @pl.when(pl.program_id(0) == 0)
    def _():
        mask_bias(bias_ref, bounds_ref, rank_ref, blocks)

    keys = key_ref[...]
    values = value_ref[...]
    for part in range(query_ref.shape[1] // 128):
        lanes = slice(128 * part, 128 * (part + 1))
        queries = query_ref[:, lanes]
        scores = contract(keys, queries, 0, 0) * (1.0 / math.sqrt(HD)) + bias_ref[:, lanes]
        row_max = jnp.max(scores, axis=0, keepdims=True)
        weights = jnp.exp(scores - row_max)
        row_sum = jnp.sum(weights, axis=0, keepdims=True)
        total_ref[0, :, lanes] = row_max + jnp.log(row_sum)
        probs = (weights * (1.0 / row_sum)).astype(bf16)
        mixed_ref[:, lanes] = contract(values, probs, 1, 0).astype(bf16)


def attend_back_kernel(
    blocks,
    rank_ref,
    bounds_ref,
    query_ref,
    key_ref,
    value_ref,
    mixed_ref,
    grad_ref,
    total_ref,
    out_ref,
    bias_ref,
    probs_ref,
    slope_ref,
):
    @pl.when(pl.program_id(0) == 0)
    def _():
        mask_bias(bias_ref, bounds_ref, rank_ref, blocks)

    keys = key_ref[...]
    values = value_ref[...]
    scale = 1.0 / math.sqrt(HD)
    for part in range(query_ref.shape[1] // 128):
        lanes = slice(128 * part, 128 * (part + 1))
        queries = query_ref[:, lanes]
        grads = grad_ref[:, lanes]
        scores = contract(keys, queries, 0, 0) * scale + bias_ref[:, lanes]
        probs = jnp.exp(scores - total_ref[0, :, lanes])
        delta = jnp.sum(grads.astype(f32) * mixed_ref[:, lanes].astype(f32), axis=0, keepdims=True)
        grad_probs = contract(values, grads, 0, 0)
        slope = (probs * (grad_probs - delta) * scale).astype(bf16)
        probs_ref[:, lanes] = probs.astype(bf16)
        slope_ref[:, lanes] = slope
        out_ref[0, :, lanes] = contract(keys, slope, 1, 0).astype(bf16)
    slope = slope_ref[...]
    out_ref[1] = contract(query_ref[...], slope, 1, 1).astype(bf16)
    out_ref[2] = contract(grad_ref[...], probs_ref[...], 1, 1).astype(bf16)


def attend(projected, bounds, rank, blocks, heads):
    seq = projected.shape[1]
    row = lambda shift: pl.BlockSpec((HD, seq), lambda h, _: (h + shift, 0))
    return pl.pallas_call(
        lambda *refs: attend_kernel(blocks, *refs),
        grid_spec=pltpu.PrefetchScalarGridSpec(
            num_scalar_prefetch=1,
            grid=(heads,),
            in_specs=[pl.BlockSpec((8, seq), lambda h, _: (0, 0)), row(0), row(heads), row(2 * heads)],
            out_specs=[row(0), pl.BlockSpec((1, 1, seq), lambda h, _: (h, 0, 0))],
            scratch_shapes=[pltpu.VMEM((seq, seq), f32)],
        ),
        out_shape=[
            jax.ShapeDtypeStruct((heads * HD, seq), bf16),
            jax.ShapeDtypeStruct((heads, 1, seq), f32),
        ],
        cost_estimate=pl.CostEstimate(
            flops=4 * heads * seq * seq * HD,
            transcendentals=heads * seq * seq,
            bytes_accessed=8 * heads * HD * seq,
        ),
        name="attend",
    )(rank.reshape(1), bounds, projected, projected, projected)


def attend_back(projected, mixed, grad_mixed, totals, bounds, rank, blocks, heads):
    seq = projected.shape[1]
    row = lambda shift: pl.BlockSpec((HD, seq), lambda h, _: (h + shift, 0))
    return pl.pallas_call(
        lambda *refs: attend_back_kernel(blocks, *refs),
        grid_spec=pltpu.PrefetchScalarGridSpec(
            num_scalar_prefetch=1,
            grid=(heads,),
            in_specs=[
                pl.BlockSpec((8, seq), lambda h, _: (0, 0)),
                row(0),
                row(heads),
                row(2 * heads),
                row(0),
                row(0),
                pl.BlockSpec((1, 1, seq), lambda h, _: (h, 0, 0)),
            ],
            out_specs=pl.BlockSpec((3, HD, seq), lambda h, _: (0, h, 0)),
            scratch_shapes=[
                pltpu.VMEM((seq, seq), f32),
                pltpu.VMEM((seq, seq), bf16),
                pltpu.VMEM((seq, seq), bf16),
            ],
        ),
        out_shape=jax.ShapeDtypeStruct((3, heads * HD, seq), bf16),
        cost_estimate=pl.CostEstimate(
            flops=10 * heads * seq * seq * HD,
            transcendentals=heads * seq * seq,
            bytes_accessed=16 * heads * HD * seq,
        ),
        name="back",
    )(rank.reshape(1), bounds, projected, projected, projected, mixed, grad_mixed, totals)


def shards(
    reps,
    size,
    tokens,
    segments,
    cotangent,
    packed_weight,
    output_weight,
    up_weight,
    down_weight,
    first_gain,
    first_shift,
    query_bias,
    value_bias,
    output_bias,
    second_gain,
    second_shift,
    hidden_bias,
    down_bias,
):
    rank = lax.axis_index(GRP)
    rep_rank = lax.axis_index(REP)
    own = D // size
    hidden_own = hidden_bias.shape[0]
    hidden_all = hidden_own * size
    count = tokens.shape[1]
    seq = segments.shape[1]

    begins = [own * g // HD for g in range(size)]
    heads = max(-(-own * (g + 1) // HD) - begins[g] for g in range(size))
    width = heads * HD
    offsets = [own * g - HD * min(b, HEADS - heads) for g, b in enumerate(begins)]
    margin = max(max(offsets), max(width - own - o for o in offsets))
    begin = first_head(rank, size)
    if begins[-1] * HD > D - width:
        begin = jnp.minimum(begin, HEADS - heads)
    offset = rank * own - HD * begin

    order = relative_order(size)
    rows_own = tokens[0]
    rows_all = group_gather(rows_own, size).astype(f32)
    row_mean, row_inv = row_stats(rows_all)
    packed_give = pack_columns(packed_weight, begins, width, rank, size)
    packed_blocks = [packed_give[0]] + [None] * (size - 1)
    for j in reversed(range(1, size)):
        packed_blocks[j] = swap(packed_give[j], GRP, size, j)
    shorts = (
        first_gain,
        first_shift,
        query_bias,
        value_bias,
        output_bias,
        second_gain,
        second_shift,
        down_bias,
    )
    small = jnp.stack(tie(shorts, packed_give))
    kinds = small.shape[0]
    small = group_gather(small, size).reshape(size, kinds, own)
    vectors = jnp.zeros((size, kinds, own), bf16)
    for i, o in enumerate(order):
        vectors = put(vectors, small[i][None], rank ^ o, 0)
    vectors = vectors.transpose(1, 0, 2).reshape(kinds, D).astype(f32)
    packed_cols = place_rows(packed_blocks, rank, jnp.zeros((), jnp.int32))

    up_sets = jnp.stack([up_weight[:, hidden_own * g : hidden_own * (g + 1)] for g in range(size)])
    flip = rep_rank & 1 if size == 4 else jnp.zeros((), jnp.int32)
    up_blocks = [pick(up_sets, rank, 0)] + [None] * (size - 1)
    if size == 4:
        route = [(r * 4 + g, r * 4 + (g ^ 2 ^ (r & 1))) for r in range(reps) for g in range(4)]
        up_blocks[2] = lax.ppermute(pick(up_sets, rank ^ 2 ^ flip, 0), (REP, GRP), route)
        up_blocks[1] = swap(pick(up_sets, rank ^ 1, 0), GRP, size, 1)
        up_blocks[3] = swap(up_blocks[2], REP, reps, 1)
    else:
        for j in range(1, size):
            up_blocks[j] = swap(pick(up_sets, rank ^ j, 0), GRP, size, j)
    up_cols = place_rows(up_blocks, rank, flip)
    grad_rows = group_gather(cotangent[0], size)
    edge_pairs = [(i, i + 1) for i in range(size - 1)]
    ahead = lax.ppermute(output_weight[own - margin :], GRP, edge_pairs)
    behind = lax.ppermute(output_weight[:margin], GRP, [(j, i) for i, j in edge_pairs])
    output_wide = cut(
        jnp.concatenate([ahead, output_weight, behind]), margin - offset, width, 0
    )
    wide_row = jnp.arange(width, dtype=jnp.int32)[:, None]
    wide_mine = (wide_row >= offset) & (wide_row < offset + own)
    output_mine = put(
        jnp.zeros((width, D), bf16), output_weight, offset, 0
    )

    segment_ids = segments[0]
    relative = lambda whole: jnp.concatenate(
        [cut(whole, (rank ^ o) * count, count, 0) for o in order]
    )
    position = relative(jnp.arange(seq, dtype=jnp.int32))
    segment_rows = relative(segment_ids)
    doc_begin = jnp.sum((segment_ids[:, None] < segment_rows[None, :]).astype(jnp.int32), axis=0)
    bounds = jnp.concatenate([doc_begin[None], position[None], jnp.zeros((6, seq), jnp.int32)])

    normal_a = ((rows_all - row_mean) * row_inv * vectors[0] + vectors[1]).astype(bf16)
    take = lambda vector: cut(vector, begin * HD, width, 0)
    packed_bias = jnp.concatenate([take(vectors[2]), jnp.zeros((width,), f32), take(vectors[3])])
    projected = (contract(packed_cols, normal_a, 0, 1) + packed_bias[:, None]).astype(bf16)
    mixed, totals = attend(projected, bounds, rank, size, heads)
    attn_part = contract(mixed, output_mine, 0, 0)
    rows_float = rows_own.astype(f32)
    residual = rows_float + group_scatter_sum(attn_part, size) + vectors[4]
    normed_second, inv_second = norm_rows(residual)
    normal_c_own = (normed_second * vectors[5] + vectors[6]).astype(bf16)
    normal_c = group_gather(normal_c_own, size)
    pre_act = contract(normal_c, up_cols, 1, 0) + hidden_bias.astype(f32)
    gelu_value, gelu_slope = gelu_parts(pre_act)
    hidden = gelu_value.astype(bf16)

    grad_hidden = contract(grad_rows, down_weight, 1, 1)
    grad_pre = (grad_hidden * gelu_slope).astype(bf16)
    grad_c_part = contract(grad_pre, up_cols, 1, 1)
    grad_c = group_scatter_sum(grad_c_part, size)
    grad_down = contract(grad_rows, hidden, 0, 0)
    grad_up = contract(grad_pre, normal_c, 0, 0)
    layer_part = contract(hidden, down_weight, 1, 0)

    share = reps // size
    row_bits, all_bits = log2(share), log2(reps)
    down_axis = lambda bit: all_bits - 1 - bit

    def step_natural(parts, bit, dtype=bf16):
        return halve_rows(add_parts(parts, dtype), bit, reps, down_axis(bit))

    def step_piece(value, bit):
        if bit < row_bits:
            return halve_rows(value, bit, reps, value.ndim - 2 - row_bits + bit)
        return halve_lanes(value, bit, reps)

    down_parts = halve_rows(natural_rows(grad_down, reps), 0, reps, down_axis(0))
    up_parts = step_piece(grad_up.reshape((2,) * row_bits + (hidden_own // share, D)), 0)

    grad_float = cotangent[0].astype(f32)
    grad_resid = grad_float + norm_back(grad_c, normed_second, inv_second, vectors[5])
    grad_attn_own = grad_resid.astype(bf16)
    grad_attn = group_gather(grad_attn_own, size)

    grad_mixed = contract(output_wide, grad_attn, 1, 1).astype(bf16)
    for step in range(1, all_bits - 1):
        down_parts = step_natural(down_parts, step)
    grad_packed_rows = attend_back(projected, mixed, grad_mixed, totals, bounds, rank, size, heads)
    grad_mine = cut(grad_packed_rows, offset, own, 1)
    grad_packed = contract(grad_mine.reshape(3 * own, seq), normal_a, 1, 0)
    packed_parts = step_piece(grad_packed.reshape((3,) + (2,) * row_bits + (own // share, D)), 0)

    down_last = step_natural(down_parts, all_bits - 1)
    for step in range(1, all_bits):
        up_parts = step_piece(add_parts(up_parts, bf16), step)

    grad_masked = jnp.where(wide_mine[None], grad_packed_rows, jnp.zeros_like(grad_packed_rows))
    grad_a_part = contract(grad_masked.reshape(3 * width, seq), packed_cols, 0, 1)
    grad_a = group_scatter_sum(grad_a_part, size)
    mixed_mine = cut(mixed, offset, own, 0)
    grad_output = contract(grad_attn, mixed_mine, 0, 1)
    out_parts = halve_rows(natural_rows(grad_output, reps), 0, reps, down_axis(0))
    for bit in range(1, all_bits):
        out_parts = step_natural(out_parts, bit)
    final_output = add_parts(out_parts, f32).reshape(D // reps, own).T
    layer_rows = residual + group_scatter_sum(layer_part, size) + vectors[7]
    normed_first, inv_first = norm_rows(rows_float)
    grad_in = grad_resid + norm_back(grad_a, normed_first, inv_first, vectors[0])

    def spread(values, length):
        return put(
            jnp.zeros((length,), f32), values, rank * values.shape[0], 0
        )

    sums = jnp.concatenate(
        [
            jnp.sum(grad_a * normed_first, axis=0),
            jnp.sum(grad_a, axis=0),
            spread(jnp.sum(grad_mine[0].astype(f32), axis=1), D),
            spread(jnp.sum(grad_mine[2].astype(f32), axis=1), D),
            jnp.sum(grad_attn_own.astype(f32), axis=0),
            jnp.sum(grad_c * normed_second, axis=0),
            jnp.sum(grad_c, axis=0),
            spread(jnp.sum(grad_pre.astype(f32), axis=0), hidden_all),
            jnp.sum(grad_float, axis=0),
        ]
    )
    sums = sum_over(sum_over(sums.reshape(-1, 128), GRP, size), REP, reps)

    for bit in range(1, all_bits):
        packed_parts = step_piece(add_parts(packed_parts, bf16), bit)
    piece = add_parts(packed_parts, bf16).reshape(3, own // share, own)
    rounds = match_rounds(reps, 3)
    table = jnp.array(rounds, jnp.int32)
    unit = rank * share + piece_of(rep_rank, reps, size)[0]
    origin = [[0] * 3 for _ in range(reps)]
    received = []
    for turn, chosen in enumerate(rounds):
        route = []
        for r in range(reps):
            row_part, lane_part = piece_of(r, reps, size)
            for g in range(size):
                v = g * share + row_part
                where = reps * chosen[v] + v
                origin[where // 3][where % 3] = turn
                route.append((r * size + g, (where // 3) * size + lane_part))
        sent = pick(piece, table[turn, unit], 0)
        received.append(lax.ppermute(sent, (REP, GRP), route))
    final_down = add_parts(down_last, f32).reshape(D // reps, hidden_own).T
    route = []
    for r in range(reps):
        row_part, lane_part = piece_of(r, reps, size)
        for g in range(size):
            route.append((r * size + g, (g * share + row_part) * size + lane_part))
    final_up = lax.ppermute(add_parts(up_parts, bf16).reshape(hidden_own // share, own), (REP, GRP), route).astype(f32).T

    received = jnp.stack(received)
    owner = jnp.array(origin, jnp.int32)[rep_rank]
    final_packed = jnp.concatenate([pick(received, owner[k], 0) for k in range(3)]).astype(f32).T

    ends = [D, 2 * D, 3 * D, 4 * D, 5 * D, 6 * D, 7 * D, 7 * D + hidden_all]
    return (
        layer_rows[None],
        grad_in[None],
        final_packed,
        final_output,
        final_up,
        final_down,
        *jnp.split(sums.reshape(-1), ends),
    )


def solution(mesh):
    in_specs = (
        P(REP, GRP, None),
        P(REP, None),
        P(REP, GRP, None),
        P(GRP, None),
        P(GRP, None),
        P(GRP, None),
        P(GRP, None),
    ) + (P(GRP),) * 9
    out_specs = (
        P(REP, GRP, None),
        P(REP, GRP, None),
        P(GRP, REP),
        P(GRP, REP),
        P(GRP, REP),
        P(GRP, REP),
    ) + (P(),) * 9

    def body(*args):
        return shards(mesh.shape[REP], mesh.shape[GRP], *args)

    return jax.shard_map(body, mesh=mesh, in_specs=in_specs, out_specs=out_specs, check_vma=False)
```

```python
import math

import jax
import jax.numpy as jnp
from jax import lax
from jax.experimental import pallas as pl
from jax.experimental.pallas import tpu as pltpu
from jax.sharding import PartitionSpec as P

D = 1088
HEADS = 17
HD = 64

GRP, REP = "grp", "rep"
epsilon = 1e-05
gelu_factor = 0.7978845608028654
masked_score = -1e30
f32 = jnp.float32
bf16 = jnp.bfloat16


def gelu_parts(pre_act):
    inner = gelu_factor * (pre_act + 0.044715 * pre_act * pre_act * pre_act)
    tanh_value = jnp.tanh(inner)
    gelu_value = 0.5 * pre_act * (1.0 + tanh_value)
    gelu_slope = 0.5 * (1.0 + tanh_value) + 0.5 * pre_act * (
        1.0 - tanh_value * tanh_value
    ) * gelu_factor * (1.0 + 3.0 * 0.044715 * pre_act * pre_act)
    return (gelu_value, gelu_slope)


def row_stats(field):
    row_mean = jnp.mean(field, axis=-1, keepdims=True)
    centered = field - row_mean
    inv_std = lax.rsqrt(jnp.mean(centered * centered, axis=-1, keepdims=True) + epsilon)
    return (row_mean, inv_std)


def norm_rows(field):
    row_mean, inv_std = row_stats(field)
    return ((field - row_mean) * inv_std, inv_std)


def norm_back(grad_out, normed, inv_std, gain_row):
    scaled = grad_out * gain_row
    return inv_std * (
        scaled
        - jnp.mean(scaled, axis=-1, keepdims=True)
        - normed * jnp.mean(scaled * normed, axis=-1, keepdims=True)
    )


def contract(left, right, left_dim, right_dim):
    return lax.dot_general(
        left, right, (((left_dim,), (right_dim,)), ((), ())), preferred_element_type=f32
    )


def swap(value, axis, size, bit):
    return lax.ppermute(value, axis, [(i, i ^ bit) for i in range(size)])


def starts_at(value, start, axis):
    starts = [0] * value.ndim
    starts[axis] = start
    return starts


def cut(value, start, length, axis):
    sizes = list(value.shape)
    sizes[axis] = length
    starts = starts_at(value, start, axis)
    return lax.dynamic_slice(value, starts, sizes, allow_negative_indices=False)


def pick(value, index, axis):
    return lax.squeeze(cut(value, index, 1, axis), (axis,))


def put(whole, part, start, axis):
    starts = starts_at(whole, start, axis)
    return lax.dynamic_update_slice(whole, part, starts, allow_negative_indices=False)


def log2(count):
    return count.bit_length() - 1


def relative_order(size):
    order = [0]
    bit = size // 2
    while bit:
        order = order + [o ^ bit for o in order]
        bit //= 2
    return order


def group_gather(value, size):
    bit = size // 2
    while bit:
        value = jnp.concatenate([value, swap(value, GRP, size, bit)])
        bit //= 2
    return value


def group_scatter_sum(value, size):
    bit = 1
    while bit < size:
        half = value.shape[0] // 2
        moved = swap(value[half:].astype(bf16), GRP, size, bit)
        value = value[:half] + moved.astype(f32)
        bit *= 2
    return value


def place_of(j, flip, size):
    return j ^ flip if 2 * j >= size else j


def place_kernel(rank_ref, flip_ref, *refs):
    out_ref = refs[-1]
    for j, ref in enumerate(refs[:-1]):
        rows = ref.shape[0]
        place = rank_ref[0] ^ place_of(j, flip_ref[0], len(refs) - 1)
        out_ref[pl.ds(pl.multiple_of(place * rows, 16), rows), :] = ref[...]


def place_rows(blocks, rank, flip):
    rows, cols = blocks[0].shape
    size = len(blocks)
    if rows % 16:
        whole = jnp.zeros((rows * size, cols), blocks[0].dtype)
        for j, block in enumerate(blocks):
            whole = put(whole, block, (rank ^ place_of(j, flip, size)) * rows, 0)
        return whole
    return pl.pallas_call(
        place_kernel,
        grid_spec=pltpu.PrefetchScalarGridSpec(
            num_scalar_prefetch=2,
            grid=(1,),
            in_specs=[pl.BlockSpec((rows, cols), lambda i, *_: (0, 0))] * size,
            out_specs=pl.BlockSpec((rows * size, cols), lambda i, *_: (0, 0)),
        ),
        out_shape=jax.ShapeDtypeStruct((rows * size, cols), blocks[0].dtype),
        cost_estimate=pl.CostEstimate(
            flops=0, transcendentals=0, bytes_accessed=4 * rows * size * cols
        ),
    )(rank.reshape(1), flip.reshape(1), *blocks)


def first_head(rank, size):
    return lax.div(rank * (D // size), HD)


def pack_kernel(width, rank_ref, source_ref, *out_refs):
    for j, out_ref in enumerate(out_refs):
        begin = first_head(rank_ref[0] ^ j, len(out_refs)) * HD
        parts = []
        for t in range(3):
            shift = D * t % 128
            start = pl.multiple_of(begin + (D * t - shift), 128)
            parts.append(source_ref[:, pl.ds(start, shift + width)][:, shift:])
        out_ref[...] = jnp.concatenate(parts, axis=1)


def pack_columns(weight, begins, width, rank, size):
    starts = [min(b * HD, D - width) for b in begins]
    if any(start % 128 or start != b * HD for start, b in zip(starts, begins)):
        sets = jnp.stack(
            [
                jnp.concatenate([weight[:, D * t + o : D * t + o + width] for t in range(3)], axis=1)
                for o in starts
            ]
        )
        return [pick(sets, rank ^ j, 0) for j in range(size)]
    rows = weight.shape[0]
    return pl.pallas_call(
        lambda *refs: pack_kernel(width, *refs),
        grid_spec=pltpu.PrefetchScalarGridSpec(
            num_scalar_prefetch=1,
            grid=(1,),
            in_specs=[pl.BlockSpec(weight.shape, lambda i, _: (0, 0))],
            out_specs=[pl.BlockSpec((rows, 3 * width), lambda i, _: (0, 0))] * size,
        ),
        out_shape=[jax.ShapeDtypeStruct((rows, 3 * width), weight.dtype)] * size,
        cost_estimate=pl.CostEstimate(
            flops=0, transcendentals=0, bytes_accessed=14 * rows * width * size
        ),
        name="pack",
    )(rank.reshape(1), weight)


def tie(values, deps):
    return lax.optimization_barrier((values, deps))[0]


def sum_over(vector, axis, count):
    bit = 1
    while bit < count:
        moved = swap(vector, axis, count, bit)
        vector = vector + moved
        bit *= 2
    return vector


def rep_bit(bit):
    return (lax.axis_index(REP) >> bit) & 1


def add_parts(parts, dtype):
    total = parts[0].astype(f32)
    for part in parts[1:]:
        total = total + part.astype(f32)
    return total.astype(dtype)


def halve_rows(value, bit, reps, axis):
    mine = rep_bit(bit)
    half = value.shape[axis] // 2
    keep = cut(value, mine * half, half, axis)
    give = cut(value, (1 - mine) * half, half, axis).astype(bf16)
    return keep, swap(give, REP, reps, 1 << bit)


def halve_lanes(value, bit, reps):
    mine = rep_bit(bit) == 1
    half = value.shape[-1] // 2
    low, high = value[..., :half], value[..., half:]
    give = jnp.where(mine, low, high).astype(bf16)
    return jnp.where(mine, high, low), swap(give, REP, reps, 1 << bit)


def natural_rows(value, reps):
    return value.reshape((2,) * log2(reps) + (value.shape[0] // reps,) + value.shape[1:])


def piece_of(rep, reps, size):
    row_part, lane_part = 0, 0
    for bit in range(log2(reps)):
        taken = (rep >> bit) & 1
        if bit < log2(reps // size):
            row_part = 2 * row_part + taken
        else:
            lane_part = 2 * lane_part + taken
    return row_part, lane_part


def match_rounds(reps, kinds):
    left = {v: set(range(kinds)) for v in range(reps)}
    rounds = []
    for _ in range(kinds):
        owner = {}

        def place(v, seen):
            for kind in sorted(left[v]):
                target = (reps * kind + v) // kinds
                if target in seen:
                    continue
                seen.add(target)
                if target not in owner or place(owner[target][0], seen):
                    owner[target] = (v, kind)
                    return True
            return False

        for v in range(reps):
            place(v, set())
        chosen = [0] * reps
        for v, kind in owner.values():
            chosen[v] = kind
            left[v].discard(kind)
        rounds.append(chosen)
    return rounds


def mask_bias(bias_ref, bounds_ref, rank_ref, blocks):
    order = relative_order(blocks)
    seq = bias_ref.shape[1]
    tokens = bias_ref.shape[0] // blocks
    chunk = 32
    begin = jnp.broadcast_to(bounds_ref[0:1, :], (chunk, seq))
    end = jnp.broadcast_to(bounds_ref[1:2, :], (chunk, seq))
    row = lax.broadcasted_iota(jnp.int32, (chunk, seq), 0)
    for block in range(blocks):

        def fill(i, carry):
            key_pos = (rank_ref[0] ^ order[block]) * tokens + i * chunk + row
            inside = (key_pos >= begin) & (key_pos <= end)
            place = pl.multiple_of(block * tokens + i * chunk, chunk)
            bias_ref[pl.ds(place, chunk), :] = jnp.where(inside, 0.0, masked_score)
            return carry

        lax.fori_loop(0, tokens // chunk, fill, 0)


def attend_kernel(blocks, rank_ref, bounds_ref, query_ref, key_ref, value_ref, mixed_ref, total_ref, bias_ref):
    @pl.when(pl.program_id(0) == 0)
    def _():
        mask_bias(bias_ref, bounds_ref, rank_ref, blocks)

    keys = key_ref[...]
    values = value_ref[...]
    for part in range(query_ref.shape[1] // 128):
        lanes = slice(128 * part, 128 * (part + 1))
        queries = query_ref[:, lanes]
        scores = contract(keys, queries, 0, 0) * (1.0 / math.sqrt(HD)) + bias_ref[:, lanes]
        row_max = jnp.max(scores, axis=0, keepdims=True)
        weights = jnp.exp(scores - row_max)
        row_sum = jnp.sum(weights, axis=0, keepdims=True)
        total_ref[0, :, lanes] = row_max + jnp.log(row_sum)
        probs = (weights * (1.0 / row_sum)).astype(bf16)
        mixed_ref[:, lanes] = contract(values, probs, 1, 0).astype(bf16)


def attend_back_kernel(
    blocks,
    rank_ref,
    bounds_ref,
    query_ref,
    key_ref,
    value_ref,
    mixed_ref,
    grad_ref,
    total_ref,
    out_ref,
    bias_ref,
    probs_ref,
    slope_ref,
):
    @pl.when(pl.program_id(0) == 0)
    def _():
        mask_bias(bias_ref, bounds_ref, rank_ref, blocks)

    keys = key_ref[...]
    values = value_ref[...]
    scale = 1.0 / math.sqrt(HD)
    for part in range(query_ref.shape[1] // 128):
        lanes = slice(128 * part, 128 * (part + 1))
        queries = query_ref[:, lanes]
        grads = grad_ref[:, lanes]
        scores = contract(keys, queries, 0, 0) * scale + bias_ref[:, lanes]
        probs = jnp.exp(scores - total_ref[0, :, lanes])
        delta = jnp.sum(grads.astype(f32) * mixed_ref[:, lanes].astype(f32), axis=0, keepdims=True)
        grad_probs = contract(values, grads, 0, 0)
        slope = (probs * (grad_probs - delta) * scale).astype(bf16)
        probs_ref[:, lanes] = probs.astype(bf16)
        slope_ref[:, lanes] = slope
        out_ref[0, :, lanes] = contract(keys, slope, 1, 0).astype(bf16)
    slope = slope_ref[...]
    out_ref[1] = contract(query_ref[...], slope, 1, 1).astype(bf16)
    out_ref[2] = contract(grad_ref[...], probs_ref[...], 1, 1).astype(bf16)


def attend(projected, bounds, rank, blocks, heads):
    seq = projected.shape[1]
    row = lambda shift: pl.BlockSpec((HD, seq), lambda h, _: (h + shift, 0))
    return pl.pallas_call(
        lambda *refs: attend_kernel(blocks, *refs),
        grid_spec=pltpu.PrefetchScalarGridSpec(
            num_scalar_prefetch=1,
            grid=(heads,),
            in_specs=[pl.BlockSpec((8, seq), lambda h, _: (0, 0)), row(0), row(heads), row(2 * heads)],
            out_specs=[row(0), pl.BlockSpec((1, 1, seq), lambda h, _: (h, 0, 0))],
            scratch_shapes=[pltpu.VMEM((seq, seq), f32)],
        ),
        out_shape=[
            jax.ShapeDtypeStruct((heads * HD, seq), bf16),
            jax.ShapeDtypeStruct((heads, 1, seq), f32),
        ],
        cost_estimate=pl.CostEstimate(
            flops=4 * heads * seq * seq * HD,
            transcendentals=heads * seq * seq,
            bytes_accessed=8 * heads * HD * seq,
        ),
        name="attend",
    )(rank.reshape(1), bounds, projected, projected, projected)


def attend_back(projected, mixed, grad_mixed, totals, bounds, rank, blocks, heads):
    seq = projected.shape[1]
    row = lambda shift: pl.BlockSpec((HD, seq), lambda h, _: (h + shift, 0))
    return pl.pallas_call(
        lambda *refs: attend_back_kernel(blocks, *refs),
        grid_spec=pltpu.PrefetchScalarGridSpec(
            num_scalar_prefetch=1,
            grid=(heads,),
            in_specs=[
                pl.BlockSpec((8, seq), lambda h, _: (0, 0)),
                row(0),
                row(heads),
                row(2 * heads),
                row(0),
                row(0),
                pl.BlockSpec((1, 1, seq), lambda h, _: (h, 0, 0)),
            ],
            out_specs=pl.BlockSpec((3, HD, seq), lambda h, _: (0, h, 0)),
            scratch_shapes=[
                pltpu.VMEM((seq, seq), f32),
                pltpu.VMEM((seq, seq), bf16),
                pltpu.VMEM((seq, seq), bf16),
            ],
        ),
        out_shape=jax.ShapeDtypeStruct((3, heads * HD, seq), bf16),
        cost_estimate=pl.CostEstimate(
            flops=10 * heads * seq * seq * HD,
            transcendentals=heads * seq * seq,
            bytes_accessed=16 * heads * HD * seq,
        ),
        name="back",
    )(rank.reshape(1), bounds, projected, projected, projected, mixed, grad_mixed, totals)


def shards(
    reps,
    size,
    tokens,
    segments,
    cotangent,
    packed_weight,
    output_weight,
    up_weight,
    down_weight,
    first_gain,
    first_shift,
    query_bias,
    value_bias,
    output_bias,
    second_gain,
    second_shift,
    hidden_bias,
    down_bias,
):
    rank = lax.axis_index(GRP)
    rep_rank = lax.axis_index(REP)
    own = D // size
    hidden_own = hidden_bias.shape[0]
    hidden_all = hidden_own * size
    count = tokens.shape[1]
    seq = segments.shape[1]

    begins = [own * g // HD for g in range(size)]
    heads = max(-(-own * (g + 1) // HD) - begins[g] for g in range(size))
    width = heads * HD
    offsets = [own * g - HD * min(b, HEADS - heads) for g, b in enumerate(begins)]
    margin = max(max(offsets), max(width - own - o for o in offsets))
    begin = first_head(rank, size)
    if begins[-1] * HD > D - width:
        begin = jnp.minimum(begin, HEADS - heads)
    offset = rank * own - HD * begin

    order = relative_order(size)
    rows_own = tokens[0]
    rows_all = group_gather(rows_own, size).astype(f32)
    row_mean, row_inv = row_stats(rows_all)
    packed_give = pack_columns(packed_weight, begins, width, rank, size)
    packed_blocks = [packed_give[0]] + [None] * (size - 1)
    for j in reversed(range(1, size)):
        packed_blocks[j] = swap(packed_give[j], GRP, size, j)
    shorts = (
        first_gain,
        first_shift,
        query_bias,
        value_bias,
        output_bias,
        second_gain,
        second_shift,
        down_bias,
    )
    small = jnp.stack(tie(shorts, packed_give))
    kinds = small.shape[0]
    small = group_gather(small, size).reshape(size, kinds, own)
    vectors = jnp.zeros((size, kinds, own), bf16)
    for i, o in enumerate(order):
        vectors = put(vectors, small[i][None], rank ^ o, 0)
    vectors = vectors.transpose(1, 0, 2).reshape(kinds, D).astype(f32)
    packed_cols = place_rows(packed_blocks, rank, jnp.zeros((), jnp.int32))

    up_sets = jnp.stack([up_weight[:, hidden_own * g : hidden_own * (g + 1)] for g in range(size)])
    flip = rep_rank & 1 if size == 4 else jnp.zeros((), jnp.int32)
    up_blocks = [pick(up_sets, rank, 0)] + [None] * (size - 1)
    if size == 4:
        route = [(r * 4 + g, r * 4 + (g ^ 2 ^ (r & 1))) for r in range(reps) for g in range(4)]
        up_blocks[2] = lax.ppermute(pick(up_sets, rank ^ 2 ^ flip, 0), (REP, GRP), route)
        up_blocks[1] = swap(pick(up_sets, rank ^ 1, 0), GRP, size, 1)
        up_blocks[3] = swap(up_blocks[2], REP, reps, 1)
    else:
        for j in range(1, size):
            up_blocks[j] = swap(pick(up_sets, rank ^ j, 0), GRP, size, j)
    up_cols = place_rows(up_blocks, rank, flip)
    grad_rows = group_gather(cotangent[0], size)
    edge_pairs = [(i, i + 1) for i in range(size - 1)]
    ahead = lax.ppermute(output_weight[own - margin :], GRP, edge_pairs)
    behind = lax.ppermute(output_weight[:margin], GRP, [(j, i) for i, j in edge_pairs])
    output_wide = cut(
        jnp.concatenate([ahead, output_weight, behind]), margin - offset, width, 0
    )
    wide_row = jnp.arange(width, dtype=jnp.int32)[:, None]
    wide_mine = (wide_row >= offset) & (wide_row < offset + own)
    output_mine = put(
        jnp.zeros((width, D), bf16), output_weight, offset, 0
    )

    segment_ids = segments[0]
    relative = lambda whole: jnp.concatenate(
        [cut(whole, (rank ^ o) * count, count, 0) for o in order]
    )
    position = relative(jnp.arange(seq, dtype=jnp.int32))
    segment_rows = relative(segment_ids)
    doc_begin = jnp.sum((segment_ids[:, None] < segment_rows[None, :]).astype(jnp.int32), axis=0)
    bounds = jnp.concatenate([doc_begin[None], position[None], jnp.zeros((6, seq), jnp.int32)])

    normal_a = ((rows_all - row_mean) * row_inv * vectors[0] + vectors[1]).astype(bf16)
    take = lambda vector: cut(vector, begin * HD, width, 0)
    packed_bias = jnp.concatenate([take(vectors[2]), jnp.zeros((width,), f32), take(vectors[3])])
    projected = (contract(packed_cols, normal_a, 0, 1) + packed_bias[:, None]).astype(bf16)
    mixed, totals = attend(projected, bounds, rank, size, heads)
    attn_part = contract(mixed, output_mine, 0, 0)
    rows_float = rows_own.astype(f32)
    residual = rows_float + group_scatter_sum(attn_part, size) + vectors[4]
    normed_second, inv_second = norm_rows(residual)
    normal_c_own = (normed_second * vectors[5] + vectors[6]).astype(bf16)
    normal_c = group_gather(normal_c_own, size)
    pre_act = contract(normal_c, up_cols, 1, 0) + hidden_bias.astype(f32)
    gelu_value, gelu_slope = gelu_parts(pre_act)
    hidden = gelu_value.astype(bf16)

    grad_hidden = contract(grad_rows, down_weight, 1, 1)
    grad_pre = (grad_hidden * gelu_slope).astype(bf16)
    grad_c_part = contract(grad_pre, up_cols, 1, 1)
    grad_c = group_scatter_sum(grad_c_part, size)
    grad_down = contract(grad_rows, hidden, 0, 0)
    grad_up = contract(grad_pre, normal_c, 0, 0)
    layer_part = contract(hidden, down_weight, 1, 0)

    share = reps // size
    row_bits, all_bits = log2(share), log2(reps)
    down_axis = lambda bit: all_bits - 1 - bit

    def step_natural(parts, bit, dtype=bf16):
        return halve_rows(add_parts(parts, dtype), bit, reps, down_axis(bit))

    def step_piece(value, bit):
        if bit < row_bits:
            return halve_rows(value, bit, reps, value.ndim - 2 - row_bits + bit)
        return halve_lanes(value, bit, reps)

    down_parts = halve_rows(natural_rows(grad_down, reps), 0, reps, down_axis(0))
    up_parts = step_piece(grad_up.reshape((2,) * row_bits + (hidden_own // share, D)), 0)

    grad_float = cotangent[0].astype(f32)
    grad_resid = grad_float + norm_back(grad_c, normed_second, inv_second, vectors[5])
    grad_attn_own = grad_resid.astype(bf16)
    grad_attn = group_gather(grad_attn_own, size)

    grad_mixed = contract(output_wide, grad_attn, 1, 1).astype(bf16)
    for step in range(1, all_bits - 1):
        down_parts = step_natural(down_parts, step)
    grad_packed_rows = attend_back(projected, mixed, grad_mixed, totals, bounds, rank, size, heads)
    grad_mine = cut(grad_packed_rows, offset, own, 1)
    grad_packed = contract(grad_mine.reshape(3 * own, seq), normal_a, 1, 0)
    packed_parts = step_piece(grad_packed.reshape((3,) + (2,) * row_bits + (own // share, D)), 0)

    down_last = step_natural(down_parts, all_bits - 1)
    for step in range(1, all_bits):
        up_parts = step_piece(add_parts(up_parts, bf16), step)

    grad_masked = jnp.where(wide_mine[None], grad_packed_rows, jnp.zeros_like(grad_packed_rows))
    grad_a_part = contract(grad_masked.reshape(3 * width, seq), packed_cols, 0, 1)
    grad_a = group_scatter_sum(grad_a_part, size)
    mixed_mine = cut(mixed, offset, own, 0)
    grad_output = contract(grad_attn, mixed_mine, 0, 1)
    out_parts = halve_rows(natural_rows(grad_output, reps), 0, reps, down_axis(0))
    for bit in range(1, all_bits):
        out_parts = step_natural(out_parts, bit)
    final_output = add_parts(out_parts, f32).reshape(D // reps, own).T
    layer_rows = residual + group_scatter_sum(layer_part, size) + vectors[7]
    normed_first, inv_first = norm_rows(rows_float)
    grad_in = grad_resid + norm_back(grad_a, normed_first, inv_first, vectors[0])

    def spread(values, length):
        return put(
            jnp.zeros((length,), f32), values, rank * values.shape[0], 0
        )

    sums = jnp.concatenate(
        [
            jnp.sum(grad_a * normed_first, axis=0),
            jnp.sum(grad_a, axis=0),
            spread(jnp.sum(grad_mine[0].astype(f32), axis=1), D),
            spread(jnp.sum(grad_mine[2].astype(f32), axis=1), D),
            jnp.sum(grad_attn_own.astype(f32), axis=0),
            jnp.sum(grad_c * normed_second, axis=0),
            jnp.sum(grad_c, axis=0),
            spread(jnp.sum(grad_pre.astype(f32), axis=0), hidden_all),
            jnp.sum(grad_float, axis=0),
        ]
    )
    sums = sum_over(sum_over(sums.reshape(-1, 128), GRP, size), REP, reps)

    for bit in range(1, all_bits):
        packed_parts = step_piece(add_parts(packed_parts, bf16), bit)
    piece = add_parts(packed_parts, bf16).reshape(3, own // share, own)
    rounds = match_rounds(reps, 3)
    table = jnp.array(rounds, jnp.int32)
    unit = rank * share + piece_of(rep_rank, reps, size)[0]
    origin = [[0] * 3 for _ in range(reps)]
    received = []
    for turn, chosen in enumerate(rounds):
        route = []
        for r in range(reps):
            row_part, lane_part = piece_of(r, reps, size)
            for g in range(size):
                v = g * share + row_part
                where = reps * chosen[v] + v
                origin[where // 3][where % 3] = turn
                route.append((r * size + g, (where // 3) * size + lane_part))
        sent = pick(piece, table[turn, unit], 0)
        received.append(lax.ppermute(sent, (REP, GRP), route))
    final_down = add_parts(down_last, f32).reshape(D // reps, hidden_own).T
    route = []
    for r in range(reps):
        row_part, lane_part = piece_of(r, reps, size)
        for g in range(size):
            route.append((r * size + g, (g * share + row_part) * size + lane_part))
    up_piece = add_parts(up_parts, bf16).reshape(hidden_own // share, own).T
    final_up = lax.ppermute(up_piece, (REP, GRP), route).astype(f32)

    received = jnp.stack(received)
    owner = jnp.array(origin, jnp.int32)[rep_rank]
    final_packed = jnp.concatenate([pick(received, owner[k], 0) for k in range(3)]).astype(f32).T

    ends = [D, 2 * D, 3 * D, 4 * D, 5 * D, 6 * D, 7 * D, 7 * D + hidden_all]
    return (
        layer_rows[None],
        grad_in[None],
        final_packed,
        final_output,
        final_up,
        final_down,
        *jnp.split(sums.reshape(-1), ends),
    )


def solution(mesh):
    in_specs = (
        P(REP, GRP, None),
        P(REP, None),
        P(REP, GRP, None),
        P(GRP, None),
        P(GRP, None),
        P(GRP, None),
        P(GRP, None),
    ) + (P(GRP),) * 9
    out_specs = (
        P(REP, GRP, None),
        P(REP, GRP, None),
        P(GRP, REP),
        P(GRP, REP),
        P(GRP, REP),
        P(GRP, REP),
    ) + (P(),) * 9

    def body(*args):
        return shards(mesh.shape[REP], mesh.shape[GRP], *args)

    return jax.shard_map(body, mesh=mesh, in_specs=in_specs, out_specs=out_specs, check_vma=False)
```
